128 devices in a mesh: tok: 8 (over z_lo, x), mem: 8 (over z_hi, y), row: 2 (over core).
Axes of the slice: x: 4, y: 4, z: 4 (z_hi: 2, z_lo: 2; z = z_hi * 2 + z_lo), core: 2. Of those that a mesh axis runs over, the one named last changes fastest.
Arguments:
- queries: bfloat16 [2, 4096, 8192], P(None, ('tok', 'row'), 'mem'), may hold values from -55 to 55
- keys: bfloat16 [2, 4096, 8192], P(None, ('tok', 'row'), 'mem'), may hold values from -3 to 3
- values: bfloat16 [2, 4096, 8192], P(None, ('tok', 'row'), 'mem'), may hold values from -6 to 6
- token_lr: float32 [16, 2, 4096], P('mem', None, ('tok', 'row')), may hold values from 0.05 to 0.5
- momentum_rate: float32 [16], P('mem'), may hold values from 0.3 to 0.9
- update_step: float32 [16], P('mem'), may hold values from 0.2 to 0.6
- fast_weights: float32 [16, 3, 512, 512], P('mem', None, 'row'), may hold values from -0.25 to 0.25
- momentum: float32 [16, 3, 512, 512], P('mem', None, 'row'), may hold values from -24 to 24
Outputs:
- mixed: bfloat16 [2, 4096, 8192], P(None, ('tok', 'row'), 'mem')
- new_weights: float32 [16, 3, 512, 512], P('mem', None, 'row')
- new_momentum: float32 [16, 3, 512, 512], P('mem', None, 'row')
The draws below stay inside these ranges and needn't reach their ends.
All inputs are finite; a program needn't handle non-finite values.
Results may differ from the reference program's by a relative error of at most 0.02.
Values may be sent and summed in bfloat16 or wider, within the bound.
A program may use at most 128 MiB of HBM per device.

```python
import math
import jax
import jax.numpy as jnp
from jax import lax

HEADS = 16
DH = 512
D = 8192
HEAD_DIM = 128
ATTN_HEADS = 64
WINDOW = 256
NS_STEPS = 2
GROUPS = 2
GROUP = 4096


def draw_pair(key):
    base = jax.random.fold_in(key, 31)
    key_a, key_b = jax.random.split(base, 2)
    total = GROUPS * GROUP
    shape = (total, D)
    queries = jnp.clip(jax.random.normal(key_a, shape, jnp.float32), -3.0, 3.0)
    keys = jnp.clip(jax.random.normal(key_b, shape, jnp.float32), -3.0, 3.0)
    return (queries.reshape(GROUPS, GROUP, D), keys.reshape(GROUPS, GROUP, D))


def draw_queries(key, part):
    return draw_pair(key)[0].astype(jnp.bfloat16)


def draw_keys(key, part):
    return draw_pair(key)[1].astype(jnp.bfloat16)


def block_scale(rng, dims, shards, low, high):
    loudness = 1.0
    for dim, blocks in shards:
        draws = jax.random.uniform(jax.random.fold_in(jax.random.fold_in(rng, 6), dim), (blocks,), jnp.float32, low / len(shards), high / len(shards))
        loudness = loudness * jnp.repeat(jnp.exp(draws), dims[dim] // blocks).reshape((-1,) + (1,) * (len(dims) - 1 - dim))
    return loudness


def noise(own_key, dims, width, most, cuts=(), kind=jnp.bfloat16):
    gain = block_scale(own_key, dims, cuts, -0.22, 0.18) if cuts else 1.0
    values = jax.random.normal(own_key, dims, jnp.float32) * width * gain
    return jnp.minimum(jnp.maximum(values, -most), most).astype(kind)


def setup_inputs(seed: int = 0) -> dict:
    arg_keys = jax.random.split(jax.random.key(seed), 9)
    return {
        "queries": draw_queries(jax.random.fold_in(arg_keys[8], 71), 0),
        "keys": draw_keys(jax.random.fold_in(arg_keys[8], 71), 0),
        "values": noise(arg_keys[2], (GROUPS, GROUP, D), 1.0, 6.0, ((1, 16), (2, 8))),
        "token_lr": jnp.clip(jnp.exp(math.log(0.5) - 2.3025851 * jax.random.uniform(arg_keys[3], (HEADS, GROUPS, GROUP), jnp.float32) ** block_scale(arg_keys[3], (HEADS, GROUPS, GROUP), ((0, 8), (2, 16)), -0.2, 0.2)), 0.05, 0.5),
        "momentum_rate": jnp.clip(0.3 + 0.59999996 * jax.random.uniform(arg_keys[4], (HEADS,), jnp.float32) ** block_scale(arg_keys[4], (HEADS,), ((0, 8),), -0.2, 0.2), 0.3, 0.9),
        "update_step": jnp.clip(0.2 + 0.400000021 * jax.random.uniform(arg_keys[5], (HEADS,), jnp.float32) ** block_scale(arg_keys[5], (HEADS,), ((0, 8),), -0.2, 0.2), 0.2, 0.6),
        "fast_weights": noise(arg_keys[6], (HEADS, 3, DH, DH), DH ** -0.5, 0.25, ((0, 8), (2, 2)), jnp.float32),
        "momentum": noise(arg_keys[7], (HEADS, 3, DH, DH), 4.0, 24.0, ((0, 8), (2, 2)), jnp.float32),
    }


quintic_one = 3.4445
quintic_two = -4.775
quintic_three = 2.0315

def unit_rows(field):
    field = field.astype(jnp.float32)
    return field * lax.rsqrt(lax.optimization_barrier(jnp.mean(field * field, axis=-1, keepdims=True)) + 1e-05)

def refine(ortho, gram):
    gram_half = gram.astype(jnp.bfloat16).astype(jnp.float32)
    square = jnp.einsum('hmde,hmef->hmdf', gram_half, gram_half)
    poly = (quintic_two * gram + quintic_three * square).astype(jnp.bfloat16).astype(jnp.float32)
    turned = jnp.einsum('hmrd,hmde->hmre', ortho.astype(jnp.float32), poly)
    return (quintic_one * ortho.astype(jnp.float32) + turned).astype(jnp.bfloat16)

def attention(queries, keys, values):
    total = GROUPS * GROUP
    seq_queries = queries.reshape(total, ATTN_HEADS, HEAD_DIM)
    padding = jnp.zeros((WINDOW, ATTN_HEADS, HEAD_DIM), jnp.bfloat16)
    seq_keys = jnp.concatenate([padding, keys.reshape(total, ATTN_HEADS, HEAD_DIM)], axis=0)
    seq_values = jnp.concatenate([padding, values.reshape(total, ATTN_HEADS, HEAD_DIM)], axis=0)
    scale = HEAD_DIM ** (-0.5)

    def block(index):
        start = index * WINDOW
        query_part = lax.dynamic_slice_in_dim(seq_queries, start, WINDOW, 0).astype(jnp.float32)
        key_part = lax.dynamic_slice_in_dim(seq_keys, start, 2 * WINDOW, 0).astype(jnp.float32)
        value_part = lax.dynamic_slice_in_dim(seq_values, start, 2 * WINDOW, 0).astype(jnp.float32)
        scores = jnp.einsum('qae,kae->aqk', query_part, key_part) * scale
        query_pos = start + jnp.arange(WINDOW, dtype=jnp.int32)
        key_pos = start - WINDOW + jnp.arange(2 * WINDOW, dtype=jnp.int32)
        offset = query_pos[:, None] - key_pos[None, :]
        allowed = (offset >= 0) & (offset < WINDOW) & (key_pos[None, :] >= 0)
        scores = jnp.where(allowed[None], scores, -1e+30)
        top = lax.optimization_barrier(jnp.max(scores, axis=-1, keepdims=True))
        expo = jnp.exp(scores - top)
        probs = (expo / lax.optimization_barrier(jnp.sum(expo, axis=-1, keepdims=True))).astype(jnp.bfloat16).astype(jnp.float32)
        result = jnp.einsum('aqk,kae->qae', probs, value_part)
        return result.reshape(WINDOW, D)
    pieces = lax.map(block, jnp.arange(total // WINDOW, dtype=jnp.int32))
    return pieces.reshape(GROUPS, GROUP, D)

def reference(queries, keys, values, token_lr, momentum_rate, update_step, fast_weights, momentum):
    attended = attention(queries, keys, values)
    weights = fast_weights
    moment = momentum
    recalls = []
    for index in range(GROUPS):
        half = weights.astype(jnp.bfloat16).astype(jnp.float32)
        gate_w = half[:, 0]
        up_w = half[:, 1]
        down_w = half[:, 2]
        query_unit = unit_rows(queries[index].reshape(GROUP, HEADS, DH)).astype(jnp.bfloat16).astype(jnp.float32)
        key_unit = unit_rows(keys[index].reshape(GROUP, HEADS, DH)).astype(jnp.bfloat16).astype(jnp.float32)
        query_gate = jnp.einsum('lhd,hdf->lhf', query_unit, gate_w)
        query_up = jnp.einsum('lhd,hdf->lhf', query_unit, up_w)
        query_hidden = (jax.nn.silu(query_gate) * query_up).astype(jnp.bfloat16).astype(jnp.float32)
        recalls.append(jnp.einsum('lhf,hfd->lhd', query_hidden, down_w).reshape(GROUP, D))
        key_gate = jnp.einsum('lhd,hdf->lhf', key_unit, gate_w)
        key_up = jnp.einsum('lhd,hdf->lhf', key_unit, up_w)
        key_hidden = (jax.nn.silu(key_gate) * key_up).astype(jnp.bfloat16).astype(jnp.float32)
        rate = jnp.transpose(token_lr[:, index, :])[:, :, None]
        value_heads = values[index].reshape(GROUP, HEADS, DH).astype(jnp.float32)
        target = (-(rate * value_heads)).astype(jnp.bfloat16).astype(jnp.float32)
        back = jnp.einsum('lhd,hfd->lhf', target, down_w)
        sig = jax.nn.sigmoid(key_gate)
        gate_in = (back * key_up * sig * (1.0 + key_gate * (1.0 - sig))).astype(jnp.bfloat16).astype(jnp.float32)
        up_in = (back * jax.nn.silu(key_gate)).astype(jnp.bfloat16).astype(jnp.float32)
        gradient = jnp.stack([jnp.einsum('lhd,lhf->hdf', key_unit, gate_in), jnp.einsum('lhd,lhf->hdf', key_unit, up_in), jnp.einsum('lhf,lhd->hfd', key_hidden, target)], axis=1)
        moment = momentum_rate[:, None, None, None] * moment + gradient
        ortho = (moment * lax.rsqrt(lax.optimization_barrier(jnp.sum(moment * moment, axis=(2, 3), keepdims=True)) + 1e-06)).astype(jnp.bfloat16)
        for turn in range(NS_STEPS):
            wide = ortho.astype(jnp.float32)
            gram = jnp.einsum('hmrd,hmre->hmde', wide, wide)
            ortho = refine(ortho, gram)
        stepped = weights - update_step[:, None, None, None] * ortho.astype(jnp.float32)
        weights = stepped * lax.rsqrt(lax.optimization_barrier(jnp.sum(stepped * stepped, axis=2, keepdims=True)) + 1e-06)
    mixed = (attended + jnp.stack(recalls, axis=0)).astype(jnp.bfloat16)
    return (mixed, weights, moment)
```

```python
import jax
import jax.numpy as jnp
from jax import lax
from jax.experimental import pallas as pl
from jax.experimental.pallas import tpu as pltpu
from jax.sharding import PartitionSpec as P

DH = 512
HEAD_DIM = 128
QUINTIC = (3.4445, -4.775, 2.0315)
MESH = pl.DeviceIdType.MESH
F32 = jnp.float32
BF16 = jnp.bfloat16
T = 256
UNITS = 12


def dot(a, b, dims=((1,), (0,))):
    return lax.dot_general(a, b, (dims, ((), ())), preferred_element_type=F32)


def unit_rows(field):
    field = field.astype(F32)
    return (field * lax.rsqrt(jnp.mean(field * field, axis=-1, keepdims=True) + 1e-05)).astype(BF16)


def kernel(
    q_in, k_in, v_in, lr_in, rate_in, step_in, w_in, m_in,
    mixed_out, w_out, m_out,
    qv, kv, vv, halo, mix, recall, w32, m32, w16, m_send, m_recv,
    left, right, send_a, recv_a, own, send_b, recv_b1, send_b2, recv_b2, total,
    ortho, gram, gram16, poly,
    load_sem, w_load, m_load, w_ssem, w_rsem, m_ssem, m_rsem, h_ssem, h_rsem,
    ssem, rsem, out_sem, mix_sem,
):
    tok = lax.axis_index("tok")
    row = lax.axis_index("row")
    x = lax.rem(tok, 4)
    z = lax.div(tok, 4)
    other = 1 - row
    z_tok = lax.rem(tok + 4, 8)
    device = tok * 2 + row
    after = lax.rem(device + 1, 16)
    before = lax.rem(device + 15, 16)
    mine = pl.multiple_of(row * T, T)
    theirs = pl.multiple_of(other * T, T)

    def chip(t):
        return {"tok": t, "row": row}

    partner = {"tok": tok, "row": other}
    z_peer = chip(z_tok)
    next_dev = {"tok": lax.div(after, 2), "row": lax.rem(after, 2)}
    prev_dev = {"tok": lax.div(before, 2), "row": lax.rem(before, 2)}

    def x_of(k):
        return lax.rem(x + k, 4)

    def x_peer(k):
        return chip(z * 4 + x_of(k))

    def remote(src, dst, send, recv, target):
        return pltpu.make_async_remote_copy(
            src_ref=src, dst_ref=dst, send_sem=send, recv_sem=recv,
            device_id=target, device_id_type=MESH,
        )

    def w_copy(i):
        return pltpu.make_async_copy(
            w_in.at[lax.div(i, 3), lax.rem(i, 3)], w32.at[i, pl.ds(mine, T)], w_load.at[i]
        )

    def m_copy(i):
        return pltpu.make_async_copy(
            m_in.at[lax.div(i, 3), lax.rem(i, 3)], m32.at[i, pl.ds(mine, T)], m_load.at[i]
        )

    k_copy = pltpu.make_async_copy(k_in, kv, load_sem.at[0])
    v_copy = pltpu.make_async_copy(v_in, vv, load_sem.at[1])
    q_copy = pltpu.make_async_copy(q_in, qv, load_sem.at[2])

    @pl.loop(0, 6)
    def _(i):
        w_copy(i).start()

    k_copy.start()
    v_copy.start()

    @pl.loop(0, 6)
    def _(i):
        m_copy(i).start()

    q_copy.start()

    barrier = pltpu.get_barrier_semaphore()
    for target in (partner, x_peer(1), x_peer(2), x_peer(3), z_peer, next_dev, prev_dev):
        pl.semaphore_signal(barrier, inc=1, device_id=target, device_id_type=MESH)
    pl.semaphore_wait(barrier, 7)

    def w_send(i):
        block = w16.at[i, pl.ds(mine, T)]
        return remote(block, block, w_ssem.at[i], w_rsem.at[i], partner)

    def m_remote(i):
        return remote(m_send.at[i], m_recv.at[i], m_ssem.at[i], m_rsem.at[i], partner)

    def halo_copy(which, c):
        source = (k_in, v_in)[which]
        return remote(
            source.at[c], halo.at[which, c], h_ssem.at[which, c], h_rsem.at[which, c], next_dev
        )

    @pl.loop(0, 6)
    def _(i):
        w_copy(i).wait()
        w16[i, pl.ds(mine, T)] = w32[i, pl.ds(mine, T)].astype(BF16)
        w_send(i).start()

    halo_copy(0, 0).start()
    halo_copy(1, 0).start()
    k_copy.wait()
    v_copy.wait()

    @pl.loop(0, 6)
    def _(i):
        m_copy(i).wait()
        m_send[i] = m32[i, pl.ds(mine, T)].astype(BF16)
        m_remote(i).start()

    q_copy.wait()

    def split(u):
        c = lax.div(u, 6)
        m = lax.rem(u, 6)
        h = lax.div(m, 3)
        jj = lax.rem(m, 3)
        return c, h, jj, h * 3 + lax.rem(jj + 2, 3), m

    row_id = lax.broadcasted_iota(jnp.int32, (T, T), 0)
    col_id = lax.broadcasted_iota(jnp.int32, (T, T), 1)

    def keys(u):
        c, h, _, _, _ = split(u)

        @pl.when(c == 0)
        def _():
            for j in range(3):
                w_send(h * 3 + j).wait_recv()

        base = c * 6 + h * 3
        lanes = pl.ds(pl.multiple_of(h * DH, DH), DH)
        unit = unit_rows(kv[c, :, lanes])
        left[1] = unit
        gate = dot(unit, w16[base])
        up = dot(unit, w16[base + 1])
        sig = jax.nn.sigmoid(gate)
        silu = gate * sig
        left[0] = (silu * up).astype(BF16)
        lr = lr_in[h, pl.ds(c, 1), :]
        lr = jnp.sum(jnp.where(row_id == col_id, lr, 0.0), axis=1, keepdims=True)
        target = (-(lr * vv[c, :, lanes].astype(F32))).astype(BF16)
        right[0] = target
        back = dot(target, w16[base + 2], ((1,), (1,)))
        right[1] = (back * up * sig * (1.0 + gate * (1.0 - sig))).astype(BF16)
        right[2] = (back * silu).astype(BF16)

    def a_copy(u):
        m = lax.rem(u, 6)
        return remote(send_a.at[m], recv_a.at[u], ssem.at[0, u], rsem.at[0, u], partner)

    def stage_a(u):
        @pl.when(lax.rem(u, 3) == 0)
        def _():
            keys(u)

        _, _, jj, _, m = split(u)
        li = jnp.minimum(jj, 1)
        rhs = right[jj]
        send_a[m] = dot(left[li, :, pl.ds(theirs, T)], rhs, ((0,), (0,))).astype(BF16)
        a_copy(u).start()
        own[m] = dot(left[li, :, pl.ds(mine, T)], rhs, ((0,), (0,)))

    def by_type(u, fn):
        even = lax.rem(u, 2) == 0

        @pl.when(even)
        def _():
            fn(True)

        @pl.when(jnp.logical_not(even))
        def _():
            fn(False)

    def wait_rows(stage, u, rows, send):
        block = total.at[u, pl.ds(0, rows)]
        copy = remote(block, block, ssem.at[stage, u], rsem.at[stage, u], partner)
        if send:
            copy.wait_send()
        else:
            copy.wait_recv()

    def stage_b1(u):
        m = lax.rem(u, 6)
        a_copy(u).wait_recv()
        summed = own[m] + recv_a[u].astype(F32)
        own[m] = summed
        send_b[m] = summed.astype(BF16)

        def go(z_first):
            if z_first:
                remote(
                    send_b.at[m, pl.ds(pl.multiple_of((1 - z) * 128, 128), 128)],
                    recv_b1.at[u, pl.ds(0, 128)], ssem.at[1, u], rsem.at[1, u], z_peer,
                ).start()
            else:
                for k in (2, 1, 3):
                    remote(
                        send_b.at[m, pl.ds(pl.multiple_of(x_of(k) * 64, 64), 64)],
                        recv_b1.at[u, pl.ds((k - 1) * 64, 64)],
                        ssem.at[1, u], rsem.at[1, u], x_peer(k),
                    ).start()

        by_type(u, go)

    def stage_b2(u):
        m = lax.rem(u, 6)

        def go(z_first):
            if z_first:
                wait_rows(1, u, 128, False)
                keep = pl.ds(pl.multiple_of(z * 128, 128), 128)
                summed = own[m, keep] + recv_b1[u, pl.ds(0, 128)].astype(F32)
                own[m, keep] = summed
                send_b2[m] = summed.astype(BF16)
                for k in (2, 1, 3):
                    remote(
                        send_b2.at[m, pl.ds(pl.multiple_of(x_of(k) * 32, 32), 32)],
                        recv_b2.at[u, pl.ds((k - 1) * 32, 32)],
                        ssem.at[2, u], rsem.at[2, u], x_peer(k),
                    ).start()
            else:
                wait_rows(1, u, 192, False)
                keep = pl.ds(pl.multiple_of(x * 64, 64), 64)
                summed = own[m, keep]
                for k in range(3):
                    summed = summed + recv_b1[u, pl.ds(k * 64, 64)].astype(F32)
                own[m, keep] = summed
                send_b2[m, pl.ds(0, 64)] = summed.astype(BF16)
                remote(
                    send_b2.at[m, pl.ds(pl.multiple_of((1 - z) * 32, 32), 32)],
                    recv_b2.at[u, pl.ds(0, 32)], ssem.at[2, u], rsem.at[2, u], z_peer,
                ).start()

        by_type(u, go)

    def stage_c1(u):
        m = lax.rem(u, 6)

        def go(z_first):
            if z_first:
                wait_rows(2, u, 96, False)
                at = z * 128 + x * 32
                count = 3
            else:
                wait_rows(2, u, 32, False)
                at = x * 64 + z * 32
                count = 1
            at = pl.multiple_of(at, 32)
            summed = own[m, pl.ds(at, 32)]
            for k in range(count):
                summed = summed + recv_b2[u, pl.ds(k * 32, 32)].astype(F32)
            place = pl.ds(pl.multiple_of(row * T + at, 32), 32)
            total[u, place] = summed.astype(BF16)
            block = total.at[u, place]
            if z_first:
                for k in (2, 1, 3):
                    remote(block, block, ssem.at[3, u], rsem.at[3, u], x_peer(k)).start()
            else:
                remote(block, block, ssem.at[3, u], rsem.at[3, u], z_peer).start()

        by_type(u, go)

    def stage_c2(u):
        def go(z_first):
            if z_first:
                wait_rows(3, u, 96, False)
                place = pl.ds(pl.multiple_of(row * T + z * 128, 128), 128)
                block = total.at[u, place]
                remote(block, block, ssem.at[4, u], rsem.at[4, u], z_peer).start()
            else:
                wait_rows(3, u, 32, False)
                place = pl.ds(pl.multiple_of(row * T + x * 64, 64), 64)
                block = total.at[u, place]
                for k in (2, 1, 3):
                    remote(block, block, ssem.at[4, u], rsem.at[4, u], x_peer(k)).start()

        by_type(u, go)

    def stage_d(u):
        by_type(u, lambda z_first: wait_rows(4, u, 128 if z_first else 192, False))
        block = total.at[u, pl.ds(mine, T)]
        remote(block, block, ssem.at[5, u], rsem.at[5, u], partner).start()

    def out_copies(i):
        h, j = lax.div(i, 3), lax.rem(i, 3)
        return (
            pltpu.make_async_copy(w32.at[i, pl.ds(mine, T)], w_out.at[h, j], out_sem.at[0, i]),
            pltpu.make_async_copy(m32.at[i, pl.ds(mine, T)], m_out.at[h, j], out_sem.at[1, i]),
        )

    def stage_n(u):
        c, h, _, i, m = split(u)
        wait_rows(5, u, T, False)

        @pl.when(c == 0)
        def _():
            m_remote(i).wait_recv()
            m32[i, pl.ds(theirs, T)] = m_recv[i].astype(F32)
            w32[i, pl.ds(theirs, T)] = w16[i, pl.ds(theirs, T)].astype(F32)

        rate = rate_in[h]
        squares = jnp.zeros((1, DH), F32)
        for b in range(4):
            rows = pl.ds(b * 128, 128)
            moment = rate * m32[i, rows] + total[u, rows].astype(F32)
            m32[i, rows] = moment
            squares = squares + jnp.sum(moment * moment, axis=0, keepdims=True)
        inverse = lax.rsqrt(jnp.sum(squares, axis=1, keepdims=True) + 1e-06)
        for b in range(4):
            rows = pl.ds(b * 128, 128)
            ortho[rows] = (m32[i, rows] * inverse).astype(BF16)
        for _ in range(2):
            for b in range(4):
                rows = pl.ds(b * 128, 128)
                part = dot(ortho[:, rows], ortho[...], ((0,), (0,)))
                gram[rows] = part
                gram16[rows] = part.astype(BF16)
            for b in range(4):
                rows = pl.ds(b * 128, 128)
                square = dot(gram16[rows], gram16[...])
                poly[rows] = (QUINTIC[1] * gram[rows] + QUINTIC[2] * square).astype(BF16)
            for b in range(4):
                rows = pl.ds(b * 128, 128)
                old = ortho[rows]
                turned = dot(old, poly[...])
                ortho[rows] = (QUINTIC[0] * old.astype(F32) + turned).astype(BF16)
        step = step_in[h]
        columns = jnp.zeros((1, DH), F32)
        for b in range(4):
            rows = pl.ds(b * 128, 128)
            stepped = w32[i, rows] - step * ortho[rows].astype(F32)
            w32[i, rows] = stepped
            columns = columns + jnp.sum(stepped * stepped, axis=0, keepdims=True)
        scale = lax.rsqrt(columns + 1e-06)
        for b in range(4):
            rows = pl.ds(b * 128, 128)
            w32[i, rows] = w32[i, rows] * scale

        @pl.when(c == 0)
        def _():
            for b in range(4):
                rows = pl.ds(b * 128, 128)
                w16[6 + i, rows] = w32[i, rows].astype(BF16)

        @pl.when(c == 1)
        def _():
            for copy in out_copies(i):
                copy.start()

        wait_rows(0, u, T, True)
        by_type(u, lambda z_first: wait_rows(1, u, 128 if z_first else 192, True))
        by_type(u, lambda z_first: wait_rows(2, u, 96 if z_first else 32, True))
        by_type(u, lambda z_first: wait_rows(3, u, 96 if z_first else 32, True))
        by_type(u, lambda z_first: wait_rows(4, u, 128 if z_first else 192, True))
        wait_rows(5, u, T, True)

    first = device == 0
    near = col_id <= row_id

    def mix_copy(c, h):
        lanes = pl.ds(pl.multiple_of(h * DH, DH), DH)
        return pltpu.make_async_copy(
            mix.at[c, :, lanes], mixed_out.at[c, :, lanes], mix_sem.at[c, h]
        )

    def fill(c, h):
        base = c * 6 + h * 3
        lanes = pl.ds(pl.multiple_of(h * DH, DH), DH)
        unit = unit_rows(qv[c, :, lanes])
        gate = dot(unit, w16[base])
        up = dot(unit, w16[base + 1])
        hidden = (gate * jax.nn.sigmoid(gate) * up).astype(BF16)
        recall[...] = dot(hidden, w16[base + 2])

        @pl.when(h == 0)
        def _():
            halo_copy(0, c).wait_recv()
            halo_copy(1, c).wait_recv()

        hc = jnp.maximum(c - first.astype(jnp.int32), 0)
        bias = jnp.where(jnp.logical_and(first, c == 0), -1e30, 0.0)
        for a in range(4):
            part = pl.ds(pl.multiple_of(h * DH + a * HEAD_DIM, HEAD_DIM), HEAD_DIM)
            query = qv[c, :, part]
            here = dot(query, kv[c, :, part], ((1,), (1,)))
            there = dot(query, halo[0, hc, :, part], ((1,), (1,)))
            scale = HEAD_DIM ** (-0.5)
            scores = jnp.where(near, here * scale, there * scale + bias)
            top = jnp.max(scores, axis=-1, keepdims=True)
            expo = jnp.exp(scores - top)
            probs = expo / jnp.sum(expo, axis=-1, keepdims=True)
            near_probs = jnp.where(near, probs, 0.0).astype(BF16)
            far_probs = jnp.where(near, 0.0, probs).astype(BF16)
            result = dot(near_probs, vv[c, :, part]) + dot(far_probs, halo[1, hc, :, part])
            local = pl.ds(a * HEAD_DIM, HEAD_DIM)
            mix[c, :, part] = (recall[:, local] + result).astype(BF16)
        mix_copy(c, h).start()

    @pl.loop(0, 21)
    def _(i):
        def at(lag, fn):
            slot = i - lag
            early = jnp.logical_and(slot >= 0, slot < 6)
            late = jnp.logical_and(slot >= 9, slot < 15)
            u = jnp.where(slot >= 9, slot - 3, slot)

            @pl.when(jnp.logical_or(early, late))
            def _():
                fn(u)

        at(0, stage_a)
        at(5, stage_d)
        at(4, stage_c2)
        at(3, stage_c1)
        at(2, stage_b2)
        at(1, stage_b1)

        @pl.when(i == 7)
        def _():
            halo_copy(0, 1).start()
            halo_copy(1, 1).start()

        fills = jnp.logical_or(
            jnp.logical_or(i == 6, i == 7), jnp.logical_or(i == 15, i == 16)
        )

        @pl.when(fills)
        def _():
            c = jnp.where(i >= 15, 1, 0)
            fill(c, i - jnp.where(i >= 15, 15, 6))

        at(6, stage_n)

    @pl.loop(0, 6)
    def _(i):
        w_send(i).wait_send()
        m_remote(i).wait_send()
        for copy in out_copies(i):
            copy.wait()

    for c in range(2):
        halo_copy(0, c).wait_send()
        halo_copy(1, c).wait_send()
        for h in range(2):
            mix_copy(c, h).wait()


def shards(queries, keys, values, token_lr, momentum_rate, update_step, fast_weights, momentum):
    hbm = pl.BlockSpec(memory_space=pl.ANY)
    vmem = pl.BlockSpec(memory_space=pltpu.VMEM)
    smem = pl.BlockSpec(memory_space=pltpu.SMEM)
    dma = pltpu.SemaphoreType.DMA
    return pl.pallas_call(
        kernel,
        out_shape=(
            jax.ShapeDtypeStruct(queries.shape, BF16),
            jax.ShapeDtypeStruct(fast_weights.shape, F32),
            jax.ShapeDtypeStruct(momentum.shape, F32),
        ),
        in_specs=[hbm, hbm, hbm, vmem, smem, smem, hbm, hbm],
        out_specs=(hbm, hbm, hbm),
        scratch_shapes=[
            pltpu.VMEM((2, T, 1024), BF16),
            pltpu.VMEM((2, T, 1024), BF16),
            pltpu.VMEM((2, T, 1024), BF16),
            pltpu.VMEM((2, 2, T, 1024), BF16),
            pltpu.VMEM((2, T, 1024), BF16),
            pltpu.VMEM((T, DH), F32),
            pltpu.VMEM((6, DH, DH), F32),
            pltpu.VMEM((6, DH, DH), F32),
            pltpu.VMEM((12, DH, DH), BF16),
            pltpu.VMEM((6, T, DH), BF16),
            pltpu.VMEM((6, T, DH), BF16),
            pltpu.VMEM((2, T, DH), BF16),
            pltpu.VMEM((3, T, DH), BF16),
            pltpu.VMEM((6, T, DH), BF16),
            pltpu.VMEM((UNITS, T, DH), BF16),
            pltpu.VMEM((6, T, DH), F32),
            pltpu.VMEM((6, T, DH), BF16),
            pltpu.VMEM((UNITS, 192, DH), BF16),
            pltpu.VMEM((6, 128, DH), BF16),
            pltpu.VMEM((UNITS, 96, DH), BF16),
            pltpu.VMEM((UNITS, DH, DH), BF16),
            pltpu.VMEM((DH, DH), BF16),
            pltpu.VMEM((DH, DH), F32),
            pltpu.VMEM((DH, DH), BF16),
            pltpu.VMEM((DH, DH), BF16),
            dma((3,)), dma((6,)), dma((6,)), dma((6,)), dma((6,)), dma((6,)), dma((6,)),
            dma((2, 2)), dma((2, 2)),
            dma((6, UNITS)), dma((6, UNITS)), dma((2, 6)), dma((2, 2)),
        ],
        compiler_params=pltpu.CompilerParams(
            collective_id=0, has_side_effects=True, vmem_limit_bytes=66_000_000
        ),
    )(queries, keys, values, token_lr, momentum_rate, update_step, fast_weights, momentum)


def solution(mesh):
    wide = P(None, ("tok", "row"), "mem")
    state = P("mem", None, "row", None)
    return jax.shard_map(
        shards,
        mesh=mesh,
        in_specs=(wide, wide, wide, P("mem", None, ("tok", "row")), P("mem"), P("mem"), state, state),
        out_specs=(wide, state, state),
        check_vma=False,
    )
```

```python
import jax
import jax.numpy as jnp
from jax import lax
from jax.experimental import pallas as pl
from jax.experimental.pallas import tpu as pltpu
from jax.sharding import PartitionSpec as P

DH = 512
HEAD_DIM = 128
QUINTIC = (3.4445, -4.775, 2.0315)
MESH = pl.DeviceIdType.MESH
F32 = jnp.float32
BF16 = jnp.bfloat16
T = 256
UNITS = 12
ZC, XC = 384, 128
ROWS_1 = (128 * ZC + 192 * XC) // DH
ROWS_2 = (96 * ZC + 32 * XC) // DH

STEPS = 59
PLAN = (
    ("H", (16777217, 0,)),
    ("A", (805306927, 226,)),
    ("B1", (4217, 1811,)),
    ("B2", (69056, 23200,)),
    ("F", (36864, 5120,)),
    ("C2", (10919936, 710656,)),
    ("D", (107282432, 6660096,)),
    ("C1", (619008, 56832,)),
    ("NA", (563347456, 14237697,)),
    ("NB", (581435392, 15368193,)),
    ("E", (234881024, 528482318,)),
)


def dot(a, b, dims=((1,), (0,))):
    return lax.dot_general(a, b, (dims, ((), ())), preferred_element_type=F32)


def unit_rows(field):
    field = field.astype(F32)
    return (field * lax.rsqrt(jnp.mean(field * field, axis=-1, keepdims=True) + 1e-05)).astype(BF16)


def kernel(
    q_in, k_in, v_in, lr_in, rate_in, step_in, w_in, m_in,
    mixed_out, w_out, m_out,
    qv, kv, vv, halo, mix, recall, w32, m32, w16, m_send, m_recv,
    left, right, send_a, recv_a, own, send_b, recv_b1, send_b2, recv_b2, total,
    ortho, gram, gram16, poly, x_send, x_recv, s_send, s_recv,
    load_sem, w_load, m_load, w_ssem, w_rsem, m_ssem, m_rsem, h_ssem, h_rsem,
    ssem, rsem, out_sem, mix_sem,
):
    tok = lax.axis_index("tok")
    row = lax.axis_index("row")
    x = lax.rem(tok, 4)
    z = lax.div(tok, 4)
    other = 1 - row
    z_tok = lax.rem(tok + 4, 8)
    device = tok * 2 + row
    after = lax.rem(device + 1, 16)
    before = lax.rem(device + 15, 16)
    mine = pl.multiple_of(row * T, T)
    theirs = pl.multiple_of(other * T, T)

    def chip(t):
        return {"tok": t, "row": row}

    partner = {"tok": tok, "row": other}
    z_peer = chip(z_tok)
    next_dev = {"tok": lax.div(after, 2), "row": lax.rem(after, 2)}
    prev_dev = {"tok": lax.div(before, 2), "row": lax.rem(before, 2)}

    def x_of(k):
        return lax.rem(x + k, 4)

    def x_peer(k):
        return chip(z * 4 + x_of(k))

    def remote(src, dst, send, recv, target):
        return pltpu.make_async_remote_copy(
            src_ref=src, dst_ref=dst, send_sem=send, recv_sem=recv,
            device_id=target, device_id_type=MESH,
        )

    def w_copy(i):
        return pltpu.make_async_copy(
            w_in.at[lax.div(i, 3), lax.rem(i, 3)], w32.at[i, pl.ds(mine, T)], w_load.at[i]
        )

    def m_copy(i):
        return pltpu.make_async_copy(
            m_in.at[lax.div(i, 3), lax.rem(i, 3)], m32.at[i, pl.ds(mine, T)], m_load.at[i]
        )

    k_copy = pltpu.make_async_copy(k_in, kv, load_sem.at[0])
    v_copy = pltpu.make_async_copy(v_in, vv, load_sem.at[1])
    q_copy = pltpu.make_async_copy(q_in, qv, load_sem.at[2])

    @pl.loop(0, 6)
    def _(i):
        w_copy(i).start()

    k_copy.start()
    v_copy.start()

    @pl.loop(0, 6)
    def _(i):
        m_copy(i).start()

    q_copy.start()

    barrier = pltpu.get_barrier_semaphore()
    for target in (partner, x_peer(1), x_peer(2), x_peer(3), z_peer, next_dev, prev_dev):
        pl.semaphore_signal(barrier, inc=1, device_id=target, device_id_type=MESH)
    pl.semaphore_wait(barrier, 7)

    def w_send(i):
        block = w16.at[i, pl.ds(mine, T)]
        return remote(block, block, w_ssem.at[i], w_rsem.at[i], partner)

    def m_remote(t):
        return remote(m_send.at[t], m_recv.at[t], m_ssem.at[t], m_rsem.at[t], partner)

    def matrix(m):
        return lax.div(m, 3) * 3 + lax.rem(lax.rem(m, 3) + 2, 3)

    def halo_copy(which, c):
        source = (k_in, v_in)[which]
        return remote(
            source.at[c], halo.at[which, c], h_ssem.at[which, c], h_rsem.at[which, c], next_dev
        )

    @pl.loop(0, 6)
    def _(i):
        w_copy(i).wait()
        w16[i, pl.ds(mine, T)] = w32[i, pl.ds(mine, T)].astype(BF16)
        w_send(i).start()

    k_copy.wait()
    v_copy.wait()

    @pl.loop(0, 6)
    def _(i):
        m_copy(i).wait()

    @pl.loop(0, 3)
    def _(t):
        m_send[t] = m32[matrix(2 * t + other), pl.ds(mine, T)].astype(BF16)
        m_remote(t).start()

    q_copy.wait()

    def split(u):
        c = lax.div(u, 6)
        m = lax.rem(u, 6)
        h = lax.div(m, 3)
        jj = lax.rem(m, 3)
        return c, h, jj, matrix(m), m

    row_id = lax.broadcasted_iota(jnp.int32, (T, T), 0)
    col_id = lax.broadcasted_iota(jnp.int32, (T, T), 1)

    def keys(u):
        c, h, _, _, _ = split(u)

        @pl.when(c == 0)
        def _():
            for j in range(3):
                w_send(h * 3 + j).wait_recv()

        base = c * 6 + h * 3
        lanes = pl.ds(pl.multiple_of(h * DH, DH), DH)
        unit = unit_rows(kv[c, :, lanes])
        left[1] = unit
        gate = dot(unit, w16[base])
        up = dot(unit, w16[base + 1])
        sig = jax.nn.sigmoid(gate)
        silu = gate * sig
        left[0] = (silu * up).astype(BF16)
        lr = lr_in[h, pl.ds(c, 1), :]
        lr = jnp.sum(jnp.where(row_id == col_id, lr, 0.0), axis=1, keepdims=True)
        target = (-(lr * vv[c, :, lanes].astype(F32))).astype(BF16)
        right[0] = target
        back = dot(target, w16[base + 2], ((1,), (1,)))
        right[1] = (back * up * sig * (1.0 + gate * (1.0 - sig))).astype(BF16)
        right[2] = (back * silu).astype(BF16)

    def a_copy(u):
        m = lax.rem(u, 6)
        return remote(send_a.at[m], recv_a.at[u], ssem.at[0, u], rsem.at[0, u], partner)

    def stage_a(u):
        @pl.when(lax.rem(u, 3) == 0)
        def _():
            keys(u)

        _, _, jj, _, m = split(u)
        li = jnp.minimum(jj, 1)
        rhs = right[jj]
        send_a[m] = dot(left[li, :, pl.ds(theirs, T)], rhs, ((0,), (0,))).astype(BF16)
        a_copy(u).start()
        own[m] = dot(left[li, :, pl.ds(mine, T)], rhs, ((0,), (0,)))

    def wait_rows(stage, u, rows, send):
        block = total.at[u, pl.ds(0, rows)]
        copy = remote(block, block, ssem.at[stage, u], rsem.at[stage, u], partner)
        if send:
            copy.wait_send()
        else:
            copy.wait_recv()

    z_cols, x_cols = pl.ds(0, ZC), pl.ds(ZC, XC)

    def stage_b1(u):
        m = lax.rem(u, 6)
        a_copy(u).wait_recv()
        summed = own[m] + recv_a[u].astype(F32)
        own[m] = summed
        send_b[m] = summed.astype(BF16)

        remote(
            send_b.at[m, pl.ds(pl.multiple_of((1 - z) * 128, 128), 128), z_cols],
            recv_b1.at[u, pl.ds(0, 128), z_cols], ssem.at[1, u], rsem.at[1, u], z_peer,
        ).start()
        for k in (2, 1, 3):
            remote(
                send_b.at[m, pl.ds(pl.multiple_of(x_of(k) * 64, 64), 64), x_cols],
                recv_b1.at[u, pl.ds((k - 1) * 64, 64), x_cols],
                ssem.at[1, u], rsem.at[1, u], x_peer(k),
            ).start()

    def stage_b2(u):
        m = lax.rem(u, 6)
        wait_rows(1, u, ROWS_1, False)
        keep = pl.ds(pl.multiple_of(z * 128, 128), 128)
        summed = own[m, keep, z_cols] + recv_b1[u, pl.ds(0, 128), z_cols].astype(F32)
        own[m, keep, z_cols] = summed
        send_b2[m, :, z_cols] = summed.astype(BF16)
        for k in (2, 1, 3):
            remote(
                send_b2.at[m, pl.ds(pl.multiple_of(x_of(k) * 32, 32), 32), z_cols],
                recv_b2.at[u, pl.ds((k - 1) * 32, 32), z_cols],
                ssem.at[2, u], rsem.at[2, u], x_peer(k),
            ).start()
        keep = pl.ds(pl.multiple_of(x * 64, 64), 64)
        summed = own[m, keep, x_cols]
        for k in range(3):
            summed = summed + recv_b1[u, pl.ds(k * 64, 64), x_cols].astype(F32)
        own[m, keep, x_cols] = summed
        send_b2[m, pl.ds(0, 64), x_cols] = summed.astype(BF16)
        remote(
            send_b2.at[m, pl.ds(pl.multiple_of((1 - z) * 32, 32), 32), x_cols],
            recv_b2.at[u, pl.ds(0, 32), x_cols], ssem.at[2, u], rsem.at[2, u], z_peer,
        ).start()

    def stage_c1(u):
        m = lax.rem(u, 6)
        wait_rows(2, u, ROWS_2, False)
        for place, cols, count in ((z * 128 + x * 32, z_cols, 3), (x * 64 + z * 32, x_cols, 1)):
            summed = own[m, pl.ds(pl.multiple_of(place, 32), 32), cols]
            for k in range(count):
                summed = summed + recv_b2[u, pl.ds(k * 32, 32), cols].astype(F32)
            at = pl.ds(pl.multiple_of(row * T + place, 32), 32)
            total[u, at, cols] = summed.astype(BF16)
            block = total.at[u, at, cols]
            for target in (x_peer(2), x_peer(1), x_peer(3)) if count == 3 else (z_peer,):
                remote(block, block, ssem.at[3, u], rsem.at[3, u], target).start()

    def stage_c2(u):
        wait_rows(3, u, ROWS_2, False)
        block = total.at[u, pl.ds(pl.multiple_of(row * T + z * 128, 128), 128), z_cols]
        remote(block, block, ssem.at[4, u], rsem.at[4, u], z_peer).start()
        block = total.at[u, pl.ds(pl.multiple_of(row * T + x * 64, 64), 64), x_cols]
        for k in (2, 1, 3):
            remote(block, block, ssem.at[4, u], rsem.at[4, u], x_peer(k)).start()

    def handles(u):
        return lax.rem(u, 2) == row

    def d_copy(u):
        block = total.at[u, pl.ds(mine, T)]
        return remote(block, block, ssem.at[5, u], rsem.at[5, u], partner)

    def stage_d(u):
        wait_rows(4, u, ROWS_1, False)

        @pl.when(jnp.logical_not(handles(u)))
        def _():
            d_copy(u).start()

    def out_copies(i):
        h, j = lax.div(i, 3), lax.rem(i, 3)
        return (
            pltpu.make_async_copy(w32.at[i, pl.ds(mine, T)], w_out.at[h, j], out_sem.at[0, i]),
            pltpu.make_async_copy(m32.at[i, pl.ds(mine, T)], m_out.at[h, j], out_sem.at[1, i]),
        )

    def newton_schulz():
        for b in range(4):
            rows = pl.ds(b * 128, 128)
            part = dot(ortho[:, rows], ortho[...], ((0,), (0,)))
            gram[rows] = part
            gram16[rows] = part.astype(BF16)
        for b in range(4):
            rows = pl.ds(b * 128, 128)
            square = dot(gram16[rows], gram16[...])
            poly[rows] = (QUINTIC[1] * gram[rows] + QUINTIC[2] * square).astype(BF16)
        for b in range(4):
            rows = pl.ds(b * 128, 128)
            old = ortho[rows]
            turned = dot(old, poly[...])
            ortho[rows] = (QUINTIC[0] * old.astype(F32) + turned).astype(BF16)

    def stage_na(u):
        c, h, _, i, m = split(u)
        rate = rate_in[h]

        @pl.when(handles(u))
        def _():
            wait_rows(5, u, T, False)

            @pl.when(c == 0)
            def _():
                t = lax.div(m, 2)
                m_remote(t).wait_recv()
                m32[i, pl.ds(theirs, T)] = m_recv[t].astype(F32)

            squares = jnp.zeros((1, DH), F32)
            for b in range(4):
                rows = pl.ds(b * 128, 128)
                moment = rate * m32[i, rows] + total[u, rows].astype(F32)
                m32[i, rows] = moment
                squares = squares + jnp.sum(moment * moment, axis=0, keepdims=True)
            inverse = lax.rsqrt(jnp.sum(squares, axis=1, keepdims=True) + 1e-06)
            for b in range(4):
                rows = pl.ds(b * 128, 128)
                ortho[rows] = (m32[i, rows] * inverse).astype(BF16)
            newton_schulz()

        @pl.when(jnp.logical_not(handles(u)))
        def _():
            rows = pl.ds(mine, T)
            m32[i, rows] = rate * m32[i, rows] + total[u, rows].astype(F32)

    def x_copy(u):
        return remote(
            x_send.at[lax.rem(u, 6)], x_recv.at[u], ssem.at[6, u], rsem.at[6, u], partner
        )

    def s_copy(u):
        return remote(
            s_send.at[lax.rem(u, 6)], s_recv.at[u], ssem.at[7, u], rsem.at[7, u], partner
        )

    def half_copy(u, i, start):
        block = w16.at[6 + i, pl.ds(start, T)]
        return remote(block, block, ssem.at[8, u], rsem.at[8, u], partner)

    def stage_nb(u):
        c, h, _, i, m = split(u)

        @pl.when(handles(u))
        def _():
            @pl.when(c == 0)
            def _():
                w32[i, pl.ds(theirs, T)] = w16[i, pl.ds(theirs, T)].astype(F32)

            newton_schulz()
            x_send[m] = ortho[pl.ds(theirs, T)]
            x_copy(u).start()
            step = step_in[h]
            columns = jnp.zeros((1, DH), F32)
            for b in range(4):
                rows = pl.ds(b * 128, 128)
                stepped = w32[i, rows] - step * ortho[rows].astype(F32)
                w32[i, rows] = stepped
                columns = columns + jnp.sum(stepped * stepped, axis=0, keepdims=True)
            scale = lax.rsqrt(columns + 1e-06)
            s_send[m] = jnp.broadcast_to(scale, (8, DH))
            s_copy(u).start()

            @pl.when(c == 0)
            def _():
                for start in (mine, theirs):
                    for b in range(2):
                        rows = pl.ds(pl.multiple_of(start + b * 128, 128), 128)
                        scaled = w32[i, rows] * scale
                        w32[i, rows] = scaled
                        w16[6 + i, rows] = scaled.astype(BF16)
                    if start is mine:
                        half_copy(u, i, mine).start()

            @pl.when(c == 1)
            def _():
                rows = pl.ds(mine, T)
                w32[i, rows] = w32[i, rows] * scale
                for copy in out_copies(i):
                    copy.start()

    def stage_e(u):
        c, h, _, i, m = split(u)

        @pl.when(jnp.logical_not(handles(u)))
        def _():
            x_copy(u).wait_recv()
            s_copy(u).wait_recv()
            rows = pl.ds(mine, T)
            scale = s_recv[u, pl.ds(0, 1), :]
            scaled = (w32[i, rows] - step_in[h] * x_recv[u].astype(F32)) * scale
            w32[i, rows] = scaled

            @pl.when(c == 0)
            def _():
                w16[6 + i, rows] = scaled.astype(BF16)
                half_copy(u, i, theirs).wait_recv()

            @pl.when(c == 1)
            def _():
                for copy in out_copies(i):
                    copy.start()

            d_copy(u).wait_send()

        @pl.when(handles(u))
        def _():
            x_copy(u).wait_send()
            s_copy(u).wait_send()

            @pl.when(c == 0)
            def _():
                half_copy(u, i, mine).wait_send()

        wait_rows(0, u, T, True)
        wait_rows(1, u, ROWS_1, True)
        wait_rows(2, u, ROWS_2, True)
        wait_rows(3, u, ROWS_2, True)
        wait_rows(4, u, ROWS_1, True)

    first = device == 0
    near = col_id <= row_id

    def mix_copy(c, h):
        lanes = pl.ds(pl.multiple_of(h * DH, DH), DH)
        return pltpu.make_async_copy(
            mix.at[c, :, lanes], mixed_out.at[c, :, lanes], mix_sem.at[c, h]
        )

    def fill(c, h):
        base = c * 6 + h * 3
        lanes = pl.ds(pl.multiple_of(h * DH, DH), DH)
        unit = unit_rows(qv[c, :, lanes])
        gate = dot(unit, w16[base])
        up = dot(unit, w16[base + 1])
        hidden = (gate * jax.nn.sigmoid(gate) * up).astype(BF16)
        recall[...] = dot(hidden, w16[base + 2])

        @pl.when(h == 0)
        def _():
            halo_copy(0, c).wait_recv()
            halo_copy(1, c).wait_recv()

        hc = jnp.maximum(c - first.astype(jnp.int32), 0)
        bias = jnp.where(jnp.logical_and(first, c == 0), -1e30, 0.0)
        for a in range(4):
            part = pl.ds(pl.multiple_of(h * DH + a * HEAD_DIM, HEAD_DIM), HEAD_DIM)
            query = qv[c, :, part]
            here = dot(query, kv[c, :, part], ((1,), (1,)))
            there = dot(query, halo[0, hc, :, part], ((1,), (1,)))
            scale = HEAD_DIM ** (-0.5)
            scores = jnp.where(near, here * scale, there * scale + bias)
            top = jnp.max(scores, axis=-1, keepdims=True)
            expo = jnp.exp(scores - top)
            probs = expo / jnp.sum(expo, axis=-1, keepdims=True)
            near_probs = jnp.where(near, probs, 0.0).astype(BF16)
            far_probs = jnp.where(near, 0.0, probs).astype(BF16)
            result = dot(near_probs, vv[c, :, part]) + dot(far_probs, halo[1, hc, :, part])
            local = pl.ds(a * HEAD_DIM, HEAD_DIM)
            mix[c, :, part] = (recall[:, local] + result).astype(BF16)
        mix_copy(c, h).start()

    def stage_h(c):
        halo_copy(0, c).start()
        halo_copy(1, c).start()

    stages = {
        "A": stage_a, "B1": stage_b1, "B2": stage_b2, "C1": stage_c1, "C2": stage_c2,
        "D": stage_d, "NA": stage_na, "NB": stage_nb, "E": stage_e, "H": stage_h,
        "F": lambda f: fill(lax.div(f, 2), lax.rem(f, 2)),
    }

    def body(i, carry):
        words, units = carry
        later_words, later_units = [], []
        for (name, plan), word, unit in zip(PLAN, words, units):
            for n in range(1, len(plan)):
                word = jnp.where(i == 30 * n, plan[n], word)
            bit = lax.rem(word, 2)

            @pl.when(bit == 1)
            def _(name=name, unit=unit):
                stages[name](unit)

            later_words.append(lax.div(word, 2))
            later_units.append(unit + bit)
        return tuple(later_words), tuple(later_units)

    start_words = tuple(jnp.int32(plan[0]) for _, plan in PLAN)
    lax.fori_loop(0, STEPS, body, (start_words, (jnp.int32(0),) * len(PLAN)))

    @pl.loop(0, 6)
    def _(i):
        w_send(i).wait_send()
        for copy in out_copies(i):
            copy.wait()

    @pl.loop(0, 3)
    def _(t):
        m_remote(t).wait_send()

    for c in range(2):
        halo_copy(0, c).wait_send()
        halo_copy(1, c).wait_send()
        for h in range(2):
            mix_copy(c, h).wait()


def shards(queries, keys, values, token_lr, momentum_rate, update_step, fast_weights, momentum):
    hbm = pl.BlockSpec(memory_space=pl.ANY)
    vmem = pl.BlockSpec(memory_space=pltpu.VMEM)
    smem = pl.BlockSpec(memory_space=pltpu.SMEM)
    dma = pltpu.SemaphoreType.DMA
    return pl.pallas_call(
        kernel,
        out_shape=(
            jax.ShapeDtypeStruct(queries.shape, BF16),
            jax.ShapeDtypeStruct(fast_weights.shape, F32),
            jax.ShapeDtypeStruct(momentum.shape, F32),
        ),
        in_specs=[hbm, hbm, hbm, vmem, smem, smem, hbm, hbm],
        out_specs=(hbm, hbm, hbm),
        scratch_shapes=[
            pltpu.VMEM((2, T, 1024), BF16),
            pltpu.VMEM((2, T, 1024), BF16),
            pltpu.VMEM((2, T, 1024), BF16),
            pltpu.VMEM((2, 2, T, 1024), BF16),
            pltpu.VMEM((2, T, 1024), BF16),
            pltpu.VMEM((T, DH), F32),
            pltpu.VMEM((6, DH, DH), F32),
            pltpu.VMEM((6, DH, DH), F32),
            pltpu.VMEM((12, DH, DH), BF16),
            pltpu.VMEM((3, T, DH), BF16),
            pltpu.VMEM((3, T, DH), BF16),
            pltpu.VMEM((2, T, DH), BF16),
            pltpu.VMEM((3, T, DH), BF16),
            pltpu.VMEM((6, T, DH), BF16),
            pltpu.VMEM((UNITS, T, DH), BF16),
            pltpu.VMEM((6, T, DH), F32),
            pltpu.VMEM((6, T, DH), BF16),
            pltpu.VMEM((UNITS, 192, DH), BF16),
            pltpu.VMEM((6, 128, DH), BF16),
            pltpu.VMEM((UNITS, 96, DH), BF16),
            pltpu.VMEM((UNITS, DH, DH), BF16),
            pltpu.VMEM((DH, DH), BF16),
            pltpu.VMEM((DH, DH), F32),
            pltpu.VMEM((DH, DH), BF16),
            pltpu.VMEM((DH, DH), BF16),
            pltpu.VMEM((6, T, DH), BF16),
            pltpu.VMEM((UNITS, T, DH), BF16),
            pltpu.VMEM((6, 8, DH), F32),
            pltpu.VMEM((UNITS, 8, DH), F32),
            dma((3,)), dma((6,)), dma((6,)), dma((6,)), dma((6,)), dma((3,)), dma((3,)),
            dma((2, 2)), dma((2, 2)),
            dma((9, UNITS)), dma((9, UNITS)), dma((2, 6)), dma((2, 2)),
        ],
        compiler_params=pltpu.CompilerParams(
            collective_id=0, has_side_effects=True, vmem_limit_bytes=66_000_000
        ),
    )(queries, keys, values, token_lr, momentum_rate, update_step, fast_weights, momentum)


def solution(mesh):
    wide = P(None, ("tok", "row"), "mem")
    state = P("mem", None, "row", None)
    return jax.shard_map(
        shards,
        mesh=mesh,
        in_specs=(wide, wide, wide, P("mem", None, ("tok", "row")), P("mem"), P("mem"), state, state),
        out_specs=(wide, state, state),
        check_vma=False,
    )
```

```python
import jax
import jax.numpy as jnp
from jax import lax
from jax.experimental import pallas as pl
from jax.experimental.pallas import tpu as pltpu
from jax.sharding import PartitionSpec as P

DH = 512
HEAD_DIM = 128
QUINTIC = (3.4445, -4.775, 2.0315)
MESH = pl.DeviceIdType.MESH
F32 = jnp.float32
BF16 = jnp.bfloat16
T = 256
UNITS = 12
ZC, XC = 256, 256
ROWS_1 = (128 * ZC + 192 * XC) // DH
ROWS_2 = (96 * ZC + 32 * XC) // DH

EARLY = 2
STEPS = 53
PLAN = (
    ("A", (629145815, 5,)),
    ("B1", (352322364, 26,)),
    ("F", (4608, 40,)),
    ("C1", (56576, 2637,)),
    ("B2", (671094672, 170,)),
    ("M", (128, 0,)),
    ("C2", (483840, 21076,)),
    ("NB", (56164352, 477696,)),
    ("D", (7114752, 107792,)),
    ("H", (1310720, 0,)),
    ("E", (240386048, 8130560,)),
    ("NA", (26886144, 221824,)),
)


def dot(a, b, dims=((1,), (0,))):
    return lax.dot_general(a, b, (dims, ((), ())), preferred_element_type=F32)


def unit_rows(field):
    field = field.astype(F32)
    return (field * lax.rsqrt(jnp.mean(field * field, axis=-1, keepdims=True) + 1e-05)).astype(BF16)


def kernel(
    q_in, k_in, v_in, lr_in, rate_in, step_in, w_in, m_in,
    mixed_out, w_out, m_out,
    qv, kv, vv, halo, recall, w32, m32, w16, m_send, m_recv,
    left, right, send_a, recv_a, own, send_b, recv_b1, send_b2, recv_b2, total,
    ortho, gram, gram16, poly, x_send, x_recv, s_send, s_recv,
    load_sem, w_load, m_load, w_ssem, w_rsem, m_ssem, m_rsem, h_ssem, h_rsem,
    ssem, rsem,
):
    tok = lax.axis_index("tok")
    row = lax.axis_index("row")
    x = lax.rem(tok, 4)
    z = lax.div(tok, 4)
    other = 1 - row
    z_tok = lax.rem(tok + 4, 8)
    device = tok * 2 + row
    after = lax.rem(device + 1, 16)
    before = lax.rem(device + 15, 16)
    mine = pl.multiple_of(row * T, T)
    theirs = pl.multiple_of(other * T, T)

    def chip(t):
        return {"tok": t, "row": row}

    partner = {"tok": tok, "row": other}
    z_peer = chip(z_tok)
    next_dev = {"tok": lax.div(after, 2), "row": lax.rem(after, 2)}
    prev_dev = {"tok": lax.div(before, 2), "row": lax.rem(before, 2)}

    def x_of(k):
        return lax.rem(x + k, 4)

    def x_peer(k):
        return chip(z * 4 + x_of(k))

    def remote(src, dst, send, recv, target):
        return pltpu.make_async_remote_copy(
            src_ref=src, dst_ref=dst, send_sem=send, recv_sem=recv,
            device_id=target, device_id_type=MESH,
        )

    def w_copy(i):
        return pltpu.make_async_copy(
            w_in.at[lax.div(i, 3), lax.rem(i, 3)], w32.at[i, pl.ds(mine, T)], w_load.at[i]
        )

    def m_copy(i):
        return pltpu.make_async_copy(
            m_in.at[lax.div(i, 3), lax.rem(i, 3)], m32.at[i, pl.ds(mine, T)], m_load.at[i]
        )

    k_copy = pltpu.make_async_copy(k_in, kv, load_sem.at[0])
    v_copy = pltpu.make_async_copy(v_in, vv, load_sem.at[1])
    q_copy = pltpu.make_async_copy(q_in, qv, load_sem.at[2])

    @pl.loop(0, 6)
    def _(i):
        w_copy(i).start()

    k_copy.start()
    v_copy.start()

    @pl.loop(0, 6)
    def _(i):
        m_copy(i).start()

    q_copy.start()

    barrier = pltpu.get_barrier_semaphore()
    for target in (partner, x_peer(1), x_peer(2), x_peer(3), z_peer, next_dev, prev_dev):
        pl.semaphore_signal(barrier, inc=1, device_id=target, device_id_type=MESH)
    pl.semaphore_wait(barrier, 7)

    def w_send(i):
        block = w16.at[i, pl.ds(mine, T)]
        return remote(block, block, w_ssem.at[i], w_rsem.at[i], partner)

    def m_remote(t):
        return remote(m_send.at[t], m_recv.at[t], m_ssem.at[t], m_rsem.at[t], partner)

    def matrix(m):
        return lax.div(m, 3) * 3 + lax.rem(lax.rem(m, 3) + 2, 3)

    def halo_copy(which, c):
        source = (k_in, v_in)[which]
        return remote(
            source.at[c], halo.at[which, c], h_ssem.at[which, c], h_rsem.at[which, c], next_dev
        )

    for n in range(EARLY):
        halo_copy(n % 2, n // 2).start()

    @pl.loop(0, 6)
    def _(i):
        w_copy(i).wait()
        w16[i, pl.ds(mine, T)] = w32[i, pl.ds(mine, T)].astype(BF16)
        w_send(i).start()

    k_copy.wait()
    v_copy.wait()
    q_copy.wait()

    def split(u):
        c = lax.div(u, 6)
        m = lax.rem(u, 6)
        h = lax.div(m, 3)
        jj = lax.rem(m, 3)
        return c, h, lax.rem(jj + 2, 3), matrix(m), m

    row_id = lax.broadcasted_iota(jnp.int32, (T, T), 0)
    col_id = lax.broadcasted_iota(jnp.int32, (T, T), 1)

    def keys(u):
        c, h, _, _, _ = split(u)

        @pl.when(c == 0)
        def _():
            for j in range(3):
                w_send(h * 3 + j).wait_recv()

        base = c * 6 + h * 3
        lanes = pl.ds(pl.multiple_of(h * DH, DH), DH)
        unit = unit_rows(kv[c, :, lanes])
        left[1] = unit
        gate = dot(unit, w16[base])
        up = dot(unit, w16[base + 1])
        sig = jax.nn.sigmoid(gate)
        silu = gate * sig
        left[0] = (silu * up).astype(BF16)
        lr = lr_in[h, pl.ds(c, 1), :]
        lr = jnp.sum(jnp.where(row_id == col_id, lr, 0.0), axis=1, keepdims=True)
        target = (-(lr * vv[c, :, lanes].astype(F32))).astype(BF16)
        right[0] = target
        back = dot(target, w16[base + 2], ((1,), (1,)))
        right[1] = (back * up * sig * (1.0 + gate * (1.0 - sig))).astype(BF16)
        right[2] = (back * silu).astype(BF16)

    def a_copy(u):
        m = lax.rem(u, 6)
        return remote(send_a.at[m], recv_a.at[u], ssem.at[0, u], rsem.at[0, u], partner)

    def stage_a(u):
        @pl.when(lax.rem(u, 3) == 0)
        def _():
            keys(u)

        m = lax.rem(u, 6)
        jj = lax.rem(m, 3)
        li = jnp.minimum(jj, 1)
        rhs = right[jj]
        send_a[m] = dot(left[li, :, pl.ds(theirs, T)], rhs, ((0,), (0,))).astype(BF16)
        a_copy(u).start()
        own[m] = dot(left[li, :, pl.ds(mine, T)], rhs, ((0,), (0,)))

    def wait_rows(stage, u, rows, send):
        block = total.at[u, pl.ds(0, rows)]
        copy = remote(block, block, ssem.at[stage, u], rsem.at[stage, u], partner)
        if send:
            copy.wait_send()
        else:
            copy.wait_recv()

    z_cols, x_cols = pl.ds(0, ZC), pl.ds(ZC, XC)

    def stage_b1(u):
        m = lax.rem(u, 6)
        a_copy(u).wait_recv()
        summed = own[m] + recv_a[u].astype(F32)
        own[m] = summed
        send_b[m] = summed.astype(BF16)

        remote(
            send_b.at[m, pl.ds(pl.multiple_of((1 - z) * 128, 128), 128), z_cols],
            recv_b1.at[u, pl.ds(0, 128), z_cols], ssem.at[1, u], rsem.at[1, u], z_peer,
        ).start()
        for k in (2, 1, 3):
            remote(
                send_b.at[m, pl.ds(pl.multiple_of(x_of(k) * 64, 64), 64), x_cols],
                recv_b1.at[u, pl.ds((k - 1) * 64, 64), x_cols],
                ssem.at[1, u], rsem.at[1, u], x_peer(k),
            ).start()

    def stage_b2(u):
        m = lax.rem(u, 6)
        wait_rows(1, u, ROWS_1, False)
        keep = pl.ds(pl.multiple_of(z * 128, 128), 128)
        summed = own[m, keep, z_cols] + recv_b1[u, pl.ds(0, 128), z_cols].astype(F32)
        own[m, keep, z_cols] = summed
        send_b2[m, :, z_cols] = summed.astype(BF16)
        for k in (2, 1, 3):
            remote(
                send_b2.at[m, pl.ds(pl.multiple_of(x_of(k) * 32, 32), 32), z_cols],
                recv_b2.at[u, pl.ds((k - 1) * 32, 32), z_cols],
                ssem.at[2, u], rsem.at[2, u], x_peer(k),
            ).start()
        keep = pl.ds(pl.multiple_of(x * 64, 64), 64)
        summed = own[m, keep, x_cols]
        for k in range(3):
            summed = summed + recv_b1[u, pl.ds(k * 64, 64), x_cols].astype(F32)
        own[m, keep, x_cols] = summed
        send_b2[m, pl.ds(0, 64), x_cols] = summed.astype(BF16)
        remote(
            send_b2.at[m, pl.ds(pl.multiple_of((1 - z) * 32, 32), 32), x_cols],
            recv_b2.at[u, pl.ds(0, 32), x_cols], ssem.at[2, u], rsem.at[2, u], z_peer,
        ).start()

    def stage_c1(u):
        m = lax.rem(u, 6)
        wait_rows(2, u, ROWS_2, False)
        for place, cols, count in ((z * 128 + x * 32, z_cols, 3), (x * 64 + z * 32, x_cols, 1)):
            summed = own[m, pl.ds(pl.multiple_of(place, 32), 32), cols]
            for k in range(count):
                summed = summed + recv_b2[u, pl.ds(k * 32, 32), cols].astype(F32)
            at = pl.ds(pl.multiple_of(row * T + place, 32), 32)
            total[u, at, cols] = summed.astype(BF16)
            block = total.at[u, at, cols]
            for target in (x_peer(2), x_peer(1), x_peer(3)) if count == 3 else (z_peer,):
                remote(block, block, ssem.at[3, u], rsem.at[3, u], target).start()

    def stage_c2(u):
        wait_rows(3, u, ROWS_2, False)
        block = total.at[u, pl.ds(pl.multiple_of(row * T + z * 128, 128), 128), z_cols]
        remote(block, block, ssem.at[4, u], rsem.at[4, u], z_peer).start()
        block = total.at[u, pl.ds(pl.multiple_of(row * T + x * 64, 64), 64), x_cols]
        for k in (2, 1, 3):
            remote(block, block, ssem.at[4, u], rsem.at[4, u], x_peer(k)).start()

    def handles(u):
        return lax.rem(u, 2) == row

    def d_copy(u):
        block = total.at[u, pl.ds(mine, T)]
        return remote(block, block, ssem.at[5, u], rsem.at[5, u], partner)

    def stage_d(u):
        wait_rows(4, u, ROWS_1, False)

        @pl.when(jnp.logical_not(handles(u)))
        def _():
            d_copy(u).start()

    def newton_schulz():
        for b in range(4):
            rows = pl.ds(b * 128, 128)
            part = dot(ortho[:, rows], ortho[...], ((0,), (0,)))
            gram[rows] = part
            gram16[rows] = part.astype(BF16)
        for b in range(4):
            rows = pl.ds(b * 128, 128)
            square = dot(gram16[rows], gram16[...])
            poly[rows] = (QUINTIC[1] * gram[rows] + QUINTIC[2] * square).astype(BF16)
        for b in range(4):
            rows = pl.ds(b * 128, 128)
            old = ortho[rows]
            turned = dot(old, poly[...])
            ortho[rows] = (QUINTIC[0] * old.astype(F32) + turned).astype(BF16)

    def stage_na(u):
        c, h, j, i, m = split(u)
        rate = rate_in[h]

        @pl.when(handles(u))
        def _():
            wait_rows(5, u, T, False)

            @pl.when(c == 0)
            def _():
                t = lax.div(m, 2)
                m_remote(t).wait_recv()
                m32[i, pl.ds(theirs, T)] = m_recv[t].astype(F32)

            squares = jnp.zeros((1, DH), F32)
            for b in range(4):
                rows = pl.ds(b * 128, 128)
                moment = rate * m32[i, rows] + total[u, rows].astype(F32)
                m32[i, rows] = moment
                squares = squares + jnp.sum(moment * moment, axis=0, keepdims=True)
            inverse = lax.rsqrt(jnp.sum(squares, axis=1, keepdims=True) + 1e-06)
            for b in range(4):
                rows = pl.ds(b * 128, 128)
                ortho[rows] = (m32[i, rows] * inverse).astype(BF16)

            @pl.when(c == 1)
            def _():
                m_out[h, j] = m32[i, pl.ds(mine, T)]

            newton_schulz()

        @pl.when(jnp.logical_not(handles(u)))
        def _():
            rows = pl.ds(mine, T)
            moment = rate * m32[i, rows] + total[u, rows].astype(F32)
            m32[i, rows] = moment

            @pl.when(c == 1)
            def _():
                m_out[h, j] = moment

    def x_copy(u):
        return remote(
            x_send.at[lax.rem(u, 6)], x_recv.at[u], ssem.at[6, u], rsem.at[6, u], partner
        )

    def s_copy(u):
        return remote(
            s_send.at[lax.rem(u, 6)], s_recv.at[u], ssem.at[7, u], rsem.at[7, u], partner
        )

    def half_copy(u, i, start):
        block = w16.at[6 + i, pl.ds(start, T)]
        return remote(block, block, ssem.at[8, u], rsem.at[8, u], partner)

    def stage_nb(u):
        c, h, j, i, m = split(u)

        @pl.when(handles(u))
        def _():
            @pl.when(c == 0)
            def _():
                w32[i, pl.ds(theirs, T)] = w16[i, pl.ds(theirs, T)].astype(F32)

            newton_schulz()
            x_send[m] = ortho[pl.ds(theirs, T)]
            x_copy(u).start()
            step = step_in[h]
            columns = jnp.zeros((1, DH), F32)
            for b in range(4):
                rows = pl.ds(b * 128, 128)
                stepped = w32[i, rows] - step * ortho[rows].astype(F32)
                w32[i, rows] = stepped
                columns = columns + jnp.sum(stepped * stepped, axis=0, keepdims=True)
            scale = lax.rsqrt(columns + 1e-06)
            s_send[m] = jnp.broadcast_to(scale, (8, DH))
            s_copy(u).start()

            @pl.when(c == 0)
            def _():
                for start in (mine, theirs):
                    for b in range(2):
                        rows = pl.ds(pl.multiple_of(start + b * 128, 128), 128)
                        scaled = w32[i, rows] * scale
                        w32[i, rows] = scaled
                        w16[6 + i, rows] = scaled.astype(BF16)
                    if start is mine:
                        half_copy(u, i, mine).start()

            @pl.when(c == 1)
            def _():
                w_out[h, j] = w32[i, pl.ds(mine, T)] * scale

    def stage_e(u):
        c, h, j, i, m = split(u)

        @pl.when(jnp.logical_not(handles(u)))
        def _():
            x_copy(u).wait_recv()
            s_copy(u).wait_recv()
            rows = pl.ds(mine, T)
            scale = s_recv[u, pl.ds(0, 1), :]
            scaled = (w32[i, rows] - step_in[h] * x_recv[u].astype(F32)) * scale

            @pl.when(c == 0)
            def _():
                w32[i, rows] = scaled
                w16[6 + i, rows] = scaled.astype(BF16)
                half_copy(u, i, theirs).wait_recv()

            @pl.when(c == 1)
            def _():
                w_out[h, j] = scaled

            d_copy(u).wait_send()

        @pl.when(handles(u))
        def _():
            x_copy(u).wait_send()
            s_copy(u).wait_send()

            @pl.when(c == 0)
            def _():
                half_copy(u, i, mine).wait_send()

        wait_rows(0, u, T, True)
        wait_rows(1, u, ROWS_1, True)
        wait_rows(2, u, ROWS_2, True)
        wait_rows(3, u, ROWS_2, True)
        wait_rows(4, u, ROWS_1, True)

    first = device == 0
    near = col_id <= row_id

    def fill(c, h):
        base = c * 6 + h * 3
        lanes = pl.ds(pl.multiple_of(h * DH, DH), DH)
        unit = unit_rows(qv[c, :, lanes])
        gate = dot(unit, w16[base])
        up = dot(unit, w16[base + 1])
        hidden = (gate * jax.nn.sigmoid(gate) * up).astype(BF16)
        recall[...] = dot(hidden, w16[base + 2])

        @pl.when(h == 0)
        def _():
            halo_copy(0, c).wait_recv()
            halo_copy(1, c).wait_recv()

        hc = jnp.maximum(c - first.astype(jnp.int32), 0)
        bias = jnp.where(jnp.logical_and(first, c == 0), -1e30, 0.0)
        for a in range(4):
            part = pl.ds(pl.multiple_of(h * DH + a * HEAD_DIM, HEAD_DIM), HEAD_DIM)
            query = qv[c, :, part]
            here = dot(query, kv[c, :, part], ((1,), (1,)))
            there = dot(query, halo[0, hc, :, part], ((1,), (1,)))
            scale = HEAD_DIM ** (-0.5)
            scores = jnp.where(near, here * scale, there * scale + bias)
            top = jnp.max(scores, axis=-1, keepdims=True)
            expo = jnp.exp(scores - top)
            probs = expo / jnp.sum(expo, axis=-1, keepdims=True)
            near_probs = jnp.where(near, probs, 0.0).astype(BF16)
            far_probs = jnp.where(near, 0.0, probs).astype(BF16)
            result = dot(near_probs, vv[c, :, part]) + dot(far_probs, halo[1, hc, :, part])
            local = pl.ds(a * HEAD_DIM, HEAD_DIM)
            mixed_out[c, :, part] = (recall[:, local] + result).astype(BF16)

    def stage_h(n):
        c = lax.div(n, 2)

        @pl.when(lax.rem(n, 2) == 0)
        def _():
            halo_copy(0, c).start()

        @pl.when(lax.rem(n, 2) == 1)
        def _():
            halo_copy(1, c).start()

    def stage_m(_):
        @pl.loop(0, 6)
        def _(i):
            m_copy(i).wait()

        @pl.loop(0, 3)
        def _(t):
            m_send[t] = m32[matrix(2 * t + other), pl.ds(mine, T)].astype(BF16)
            m_remote(t).start()

    stages = {
        "A": stage_a, "B1": stage_b1, "B2": stage_b2, "C1": stage_c1, "C2": stage_c2,
        "D": stage_d, "NA": stage_na, "NB": stage_nb, "E": stage_e, "H": stage_h, "M": stage_m,
        "F": lambda f: fill(lax.div(f, 2), lax.rem(f, 2)),
    }

    def body(i, carry):
        words, units = carry
        later_words, later_units = [], []
        for (name, plan), word, unit in zip(PLAN, words, units):
            for n in range(1, len(plan)):
                word = jnp.where(i == 30 * n, plan[n], word)
            bit = lax.rem(word, 2)

            @pl.when(bit == 1)
            def _(name=name, unit=unit):
                stages[name](unit)

            later_words.append(lax.div(word, 2))
            later_units.append(unit + bit)
        return tuple(later_words), tuple(later_units)

    start_words = tuple(jnp.int32(plan[0]) for _, plan in PLAN)
    starts = tuple(jnp.int32(EARLY if name == "H" else 0) for name, _ in PLAN)
    lax.fori_loop(0, STEPS, body, (start_words, starts))

    @pl.loop(0, 6)
    def _(i):
        w_send(i).wait_send()

    @pl.loop(0, 3)
    def _(t):
        m_remote(t).wait_send()

    for c in range(2):
        halo_copy(0, c).wait_send()
        halo_copy(1, c).wait_send()


def shards(queries, keys, values, token_lr, momentum_rate, update_step, fast_weights, momentum):
    hbm = pl.BlockSpec(memory_space=pl.ANY)
    vmem = pl.BlockSpec(memory_space=pltpu.VMEM)
    smem = pl.BlockSpec(memory_space=pltpu.SMEM)
    dma = pltpu.SemaphoreType.DMA
    return pl.pallas_call(
        kernel,
        out_shape=(
            pltpu.VMEM(queries.shape, BF16),
            pltpu.VMEM(fast_weights.shape, F32),
            pltpu.VMEM(momentum.shape, F32),
        ),
        in_specs=[hbm, hbm, hbm, vmem, smem, smem, hbm, hbm],
        out_specs=(vmem, vmem, vmem),
        scratch_shapes=[
            pltpu.VMEM((2, T, 1024), BF16),
            pltpu.VMEM((2, T, 1024), BF16),
            pltpu.VMEM((2, T, 1024), BF16),
            pltpu.VMEM((2, 2, T, 1024), BF16),
            pltpu.VMEM((T, DH), F32),
            pltpu.VMEM((6, DH, DH), F32),
            pltpu.VMEM((6, DH, DH), F32),
            pltpu.VMEM((12, DH, DH), BF16),
            pltpu.VMEM((3, T, DH), BF16),
            pltpu.VMEM((3, T, DH), BF16),
            pltpu.VMEM((2, T, DH), BF16),
            pltpu.VMEM((3, T, DH), BF16),
            pltpu.VMEM((6, T, DH), BF16),
            pltpu.VMEM((UNITS, T, DH), BF16),
            pltpu.VMEM((6, T, DH), F32),
            pltpu.VMEM((6, T, DH), BF16),
            pltpu.VMEM((UNITS, 192, DH), BF16),
            pltpu.VMEM((6, 128, DH), BF16),
            pltpu.VMEM((UNITS, 96, DH), BF16),
            pltpu.VMEM((UNITS, DH, DH), BF16),
            pltpu.VMEM((DH, DH), BF16),
            pltpu.VMEM((DH, DH), F32),
            pltpu.VMEM((DH, DH), BF16),
            pltpu.VMEM((DH, DH), BF16),
            pltpu.VMEM((6, T, DH), BF16),
            pltpu.VMEM((UNITS, T, DH), BF16),
            pltpu.VMEM((6, 8, DH), F32),
            pltpu.VMEM((UNITS, 8, DH), F32),
            dma((3,)), dma((6,)), dma((6,)), dma((6,)), dma((6,)), dma((3,)), dma((3,)),
            dma((2, 2)), dma((2, 2)),
            dma((9, UNITS)), dma((9, UNITS)),
        ],
        compiler_params=pltpu.CompilerParams(
            collective_id=0, has_side_effects=True, vmem_limit_bytes=58_700_000
        ),
    )(queries, keys, values, token_lr, momentum_rate, update_step, fast_weights, momentum)


def solution(mesh):
    wide = P(None, ("tok", "row"), "mem")
    state = P("mem", None, "row", None)
    return jax.shard_map(
        shards,
        mesh=mesh,
        in_specs=(wide, wide, wide, P("mem", None, ("tok", "row")), P("mem"), P("mem"), state, state),
        out_specs=(wide, state, state),
        check_vma=False,
    )
```

```python
import jax
import jax.numpy as jnp
from jax import lax
from jax.experimental import pallas as pl
from jax.experimental.pallas import tpu as pltpu
from jax.sharding import PartitionSpec as P

DH = 512
HEAD_DIM = 128
QUINTIC = (3.4445, -4.775, 2.0315)
MESH = pl.DeviceIdType.MESH
F32 = jnp.float32
BF16 = jnp.bfloat16
T = 256
UNITS = 12
ZC, XC = 256, 256
ROWS_1 = (128 * ZC + 192 * XC) // DH
ROWS_2 = (96 * ZC + 32 * XC) // DH

EARLY = 8
STEPS = 59
PLAN = (
    ("E", (117440512, 521142314,)),
    ("M", (131072, 0,)),
    ("B2", (133056, 26646,)),
    ("C2", (151343104, 873472,)),
    ("A", (738197791, 608,)),
    ("F", (8320, 5120,)),
    ("D", (816087040, 7114752,)),
    ("NA", (576847872, 14303233,)),
    ("H", (152895488, 9,)),
    ("B1", (939528316, 2432,)),
    ("C1", (4279552, 90720,)),
    ("NB", (816054272, 15532033,)),
)


def dot(a, b, dims=((1,), (0,))):
    return lax.dot_general(a, b, (dims, ((), ())), preferred_element_type=F32)


def unit_rows(field):
    field = field.astype(F32)
    return (field * lax.rsqrt(jnp.mean(field * field, axis=-1, keepdims=True) + 1e-05)).astype(BF16)


def kernel(
    q_in, k_in, v_in, lr_in, rate_in, step_in, w_in, m_in,
    mixed_out, w_out, m_out,
    qv, kv, vv, halo, recall, w32, m32, w16, m_send, m_recv,
    left, right, send_a, recv_a, own, send_b, recv_b1, send_b2, recv_b2, total,
    ortho, gram, gram16, poly, x_send, x_recv, s_send, s_recv,
    load_sem, w_load, m_load, w_ssem, w_rsem, m_ssem, m_rsem, h_ssem, h_rsem,
    ssem, rsem,
):
    tok = lax.axis_index("tok")
    row = lax.axis_index("row")
    x = lax.rem(tok, 4)
    z = lax.div(tok, 4)
    other = 1 - row
    z_tok = lax.rem(tok + 4, 8)
    device = tok * 2 + row
    after = lax.rem(device + 1, 16)
    before = lax.rem(device + 15, 16)
    mine = pl.multiple_of(row * T, T)
    theirs = pl.multiple_of(other * T, T)

    def chip(t):
        return {"tok": t, "row": row}

    partner = {"tok": tok, "row": other}
    z_peer = chip(z_tok)
    next_dev = {"tok": lax.div(after, 2), "row": lax.rem(after, 2)}
    prev_dev = {"tok": lax.div(before, 2), "row": lax.rem(before, 2)}

    def x_of(k):
        return lax.rem(x + k, 4)

    def x_peer(k):
        return chip(z * 4 + x_of(k))

    def remote(src, dst, send, recv, target):
        return pltpu.make_async_remote_copy(
            src_ref=src, dst_ref=dst, send_sem=send, recv_sem=recv,
            device_id=target, device_id_type=MESH,
        )

    barrier = pltpu.get_barrier_semaphore()
    for target in (partner, x_peer(1), x_peer(2), x_peer(3), z_peer, next_dev, prev_dev):
        pl.semaphore_signal(barrier, inc=1, device_id=target, device_id_type=MESH)

    def w_copy(i):
        return pltpu.make_async_copy(
            w_in.at[lax.div(i, 3), lax.rem(i, 3)], w32.at[i, pl.ds(mine, T)], w_load.at[i]
        )

    def m_copy(i):
        return pltpu.make_async_copy(
            m_in.at[lax.div(i, 3), lax.rem(i, 3)], m32.at[i, pl.ds(mine, T)], m_load.at[i]
        )

    k_copy = pltpu.make_async_copy(k_in, kv, load_sem.at[0])
    v_copy = pltpu.make_async_copy(v_in, vv, load_sem.at[1])
    q_copy = pltpu.make_async_copy(q_in, qv, load_sem.at[2])

    @pl.loop(0, 6)
    def _(i):
        w_copy(i).start()

    k_copy.start()
    v_copy.start()

    @pl.loop(0, 6)
    def _(i):
        m_copy(i).start()

    q_copy.start()

    pl.semaphore_wait(barrier, 7)

    def w_send(i):
        block = w16.at[i, pl.ds(mine, T)]
        return remote(block, block, w_ssem.at[i], w_rsem.at[i], partner)

    def m_remote(t):
        return remote(m_send.at[t], m_recv.at[t], m_ssem.at[t], m_rsem.at[t], partner)

    def matrix(m):
        return lax.div(m, 3) * 3 + lax.rem(lax.rem(m, 3) + 2, 3)

    def halo_copy(n, which):
        c = lax.div(n, 8)
        source = (k_in, v_in)[which]
        rows = pl.ds(pl.multiple_of(lax.rem(lax.div(n, 2), 4) * 64, 64), 64)
        return remote(
            source.at[c, rows], halo.at[which, c, rows], h_ssem.at[n], h_rsem.at[n], next_dev
        )

    for n in range(EARLY):
        halo_copy(jnp.int32(n), n % 2).start()

    @pl.loop(0, 6)
    def _(i):
        w_copy(i).wait()
        w16[i, pl.ds(mine, T)] = w32[i, pl.ds(mine, T)].astype(BF16)
        w_send(i).start()

    k_copy.wait()
    v_copy.wait()
    q_copy.wait()

    def split(u):
        c = lax.div(u, 6)
        m = lax.rem(u, 6)
        h = lax.div(m, 3)
        jj = lax.rem(m, 3)
        return c, h, lax.rem(jj + 2, 3), matrix(m), m

    row_id = lax.broadcasted_iota(jnp.int32, (T, T), 0)
    col_id = lax.broadcasted_iota(jnp.int32, (T, T), 1)

    def keys(u):
        c, h, _, _, _ = split(u)

        @pl.when(c == 0)
        def _():
            for j in range(3):
                w_send(h * 3 + j).wait_recv()

        base = c * 6 + h * 3
        lanes = pl.ds(pl.multiple_of(h * DH, DH), DH)
        unit = unit_rows(kv[c, :, lanes])
        left[1] = unit
        gate = dot(unit, w16[base])
        up = dot(unit, w16[base + 1])
        sig = jax.nn.sigmoid(gate)
        silu = gate * sig
        left[0] = (silu * up).astype(BF16)
        lr = lr_in[h, pl.ds(c, 1), :]
        lr = jnp.sum(jnp.where(row_id == col_id, lr, 0.0), axis=1, keepdims=True)
        target = (-(lr * vv[c, :, lanes].astype(F32))).astype(BF16)
        right[0] = target
        back = dot(target, w16[base + 2], ((1,), (1,)))
        right[1] = (back * up * sig * (1.0 + gate * (1.0 - sig))).astype(BF16)
        right[2] = (back * silu).astype(BF16)

    def a_copy(u):
        m = lax.rem(u, 6)
        return remote(send_a.at[m], recv_a.at[u], ssem.at[0, u], rsem.at[0, u], partner)

    def stage_a(u):
        @pl.when(lax.rem(u, 3) == 0)
        def _():
            keys(u)

        m = lax.rem(u, 6)
        jj = lax.rem(m, 3)
        li = jnp.minimum(jj, 1)
        rhs = right[jj]
        send_a[m] = dot(left[li, :, pl.ds(theirs, T)], rhs, ((0,), (0,))).astype(BF16)
        a_copy(u).start()
        own[m] = dot(left[li, :, pl.ds(mine, T)], rhs, ((0,), (0,)))

    def wait_rows(stage, u, rows, send):
        block = total.at[u, pl.ds(0, rows)]
        copy = remote(block, block, ssem.at[stage, u], rsem.at[stage, u], partner)
        if send:
            copy.wait_send()
        else:
            copy.wait_recv()

    z_cols, x_cols = pl.ds(0, ZC), pl.ds(ZC, XC)

    def stage_b1(u):
        m = lax.rem(u, 6)
        a_copy(u).wait_recv()
        summed = own[m] + recv_a[u].astype(F32)
        own[m] = summed
        send_b[m] = summed.astype(BF16)

        remote(
            send_b.at[m, pl.ds(pl.multiple_of((1 - z) * 128, 128), 128), z_cols],
            recv_b1.at[u, pl.ds(0, 128), z_cols], ssem.at[1, u], rsem.at[1, u], z_peer,
        ).start()
        for k in (2, 1, 3):
            remote(
                send_b.at[m, pl.ds(pl.multiple_of(x_of(k) * 64, 64), 64), x_cols],
                recv_b1.at[u, pl.ds((k - 1) * 64, 64), x_cols],
                ssem.at[1, u], rsem.at[1, u], x_peer(k),
            ).start()

    def stage_b2(u):
        m = lax.rem(u, 6)
        wait_rows(1, u, ROWS_1, False)
        keep = pl.ds(pl.multiple_of(z * 128, 128), 128)
        summed = own[m, keep, z_cols] + recv_b1[u, pl.ds(0, 128), z_cols].astype(F32)
        own[m, keep, z_cols] = summed
        send_b2[m, :, z_cols] = summed.astype(BF16)
        for k in (2, 1, 3):
            remote(
                send_b2.at[m, pl.ds(pl.multiple_of(x_of(k) * 32, 32), 32), z_cols],
                recv_b2.at[u, pl.ds((k - 1) * 32, 32), z_cols],
                ssem.at[2, u], rsem.at[2, u], x_peer(k),
            ).start()
        keep = pl.ds(pl.multiple_of(x * 64, 64), 64)
        summed = own[m, keep, x_cols]
        for k in range(3):
            summed = summed + recv_b1[u, pl.ds(k * 64, 64), x_cols].astype(F32)
        own[m, keep, x_cols] = summed
        send_b2[m, pl.ds(0, 64), x_cols] = summed.astype(BF16)
        remote(
            send_b2.at[m, pl.ds(pl.multiple_of((1 - z) * 32, 32), 32), x_cols],
            recv_b2.at[u, pl.ds(0, 32), x_cols], ssem.at[2, u], rsem.at[2, u], z_peer,
        ).start()

    def stage_c1(u):
        m = lax.rem(u, 6)
        wait_rows(2, u, ROWS_2, False)
        for place, cols, count in ((z * 128 + x * 32, z_cols, 3), (x * 64 + z * 32, x_cols, 1)):
            summed = own[m, pl.ds(pl.multiple_of(place, 32), 32), cols]
            for k in range(count):
                summed = summed + recv_b2[u, pl.ds(k * 32, 32), cols].astype(F32)
            at = pl.ds(pl.multiple_of(row * T + place, 32), 32)
            total[u, at, cols] = summed.astype(BF16)
            block = total.at[u, at, cols]
            for target in (x_peer(2), x_peer(1), x_peer(3)) if count == 3 else (z_peer,):
                remote(block, block, ssem.at[3, u], rsem.at[3, u], target).start()

    def stage_c2(u):
        wait_rows(3, u, ROWS_2, False)
        block = total.at[u, pl.ds(pl.multiple_of(row * T + z * 128, 128), 128), z_cols]
        remote(block, block, ssem.at[4, u], rsem.at[4, u], z_peer).start()
        block = total.at[u, pl.ds(pl.multiple_of(row * T + x * 64, 64), 64), x_cols]
        for k in (2, 1, 3):
            remote(block, block, ssem.at[4, u], rsem.at[4, u], x_peer(k)).start()

    def handles(u):
        return lax.rem(u, 2) == row

    def d_copy(u):
        block = total.at[u, pl.ds(mine, T)]
        return remote(block, block, ssem.at[5, u], rsem.at[5, u], partner)

    def stage_d(u):
        wait_rows(4, u, ROWS_1, False)

        @pl.when(jnp.logical_not(handles(u)))
        def _():
            d_copy(u).start()

    def newton_schulz():
        for b in range(4):
            rows = pl.ds(b * 128, 128)
            part = dot(ortho[:, rows], ortho[...], ((0,), (0,)))
            gram[rows] = part
            gram16[rows] = part.astype(BF16)
        for b in range(4):
            rows = pl.ds(b * 128, 128)
            square = dot(gram16[rows], gram16[...])
            poly[rows] = (QUINTIC[1] * gram[rows] + QUINTIC[2] * square).astype(BF16)
        for b in range(4):
            rows = pl.ds(b * 128, 128)
            old = ortho[rows]
            turned = dot(old, poly[...])
            ortho[rows] = (QUINTIC[0] * old.astype(F32) + turned).astype(BF16)

    def stage_na(u):
        c, h, j, i, m = split(u)
        rate = rate_in[h]

        @pl.when(handles(u))
        def _():
            wait_rows(5, u, T, False)

            @pl.when(c == 0)
            def _():
                t = lax.div(m, 2)
                m_remote(t).wait_recv()
                m32[i, pl.ds(theirs, T)] = m_recv[t].astype(F32)

            squares = jnp.zeros((1, DH), F32)
            for b in range(4):
                rows = pl.ds(b * 128, 128)
                moment = rate * m32[i, rows] + total[u, rows].astype(F32)
                m32[i, rows] = moment
                squares = squares + jnp.sum(moment * moment, axis=0, keepdims=True)
            inverse = lax.rsqrt(jnp.sum(squares, axis=1, keepdims=True) + 1e-06)
            for b in range(4):
                rows = pl.ds(b * 128, 128)
                ortho[rows] = (m32[i, rows] * inverse).astype(BF16)

            @pl.when(c == 1)
            def _():
                m_out[h, j] = m32[i, pl.ds(mine, T)]

            newton_schulz()

        @pl.when(jnp.logical_not(handles(u)))
        def _():
            rows = pl.ds(mine, T)
            moment = rate * m32[i, rows] + total[u, rows].astype(F32)
            m32[i, rows] = moment

            @pl.when(c == 1)
            def _():
                m_out[h, j] = moment

    def x_copy(u):
        return remote(
            x_send.at[lax.rem(u, 6)], x_recv.at[u], ssem.at[6, u], rsem.at[6, u], partner
        )

    def s_copy(u):
        return remote(
            s_send.at[lax.rem(u, 6)], s_recv.at[u], ssem.at[7, u], rsem.at[7, u], partner
        )

    def half_copy(u, i, start):
        block = w16.at[6 + i, pl.ds(start, T)]
        return remote(block, block, ssem.at[8, u], rsem.at[8, u], partner)

    def stage_nb(u):
        c, h, j, i, m = split(u)

        @pl.when(handles(u))
        def _():
            @pl.when(c == 0)
            def _():
                w32[i, pl.ds(theirs, T)] = w16[i, pl.ds(theirs, T)].astype(F32)

            newton_schulz()
            x_send[m] = ortho[pl.ds(theirs, T)]
            x_copy(u).start()
            step = step_in[h]
            columns = jnp.zeros((1, DH), F32)
            for b in range(4):
                rows = pl.ds(b * 128, 128)
                stepped = w32[i, rows] - step * ortho[rows].astype(F32)
                w32[i, rows] = stepped
                columns = columns + jnp.sum(stepped * stepped, axis=0, keepdims=True)
            scale = lax.rsqrt(columns + 1e-06)
            s_send[m] = jnp.broadcast_to(scale, (8, DH))
            s_copy(u).start()

            @pl.when(c == 0)
            def _():
                for start in (mine, theirs):
                    for b in range(2):
                        rows = pl.ds(pl.multiple_of(start + b * 128, 128), 128)
                        scaled = w32[i, rows] * scale
                        w32[i, rows] = scaled
                        w16[6 + i, rows] = scaled.astype(BF16)
                    if start is mine:
                        half_copy(u, i, mine).start()

            @pl.when(c == 1)
            def _():
                w_out[h, j] = w32[i, pl.ds(mine, T)] * scale

    def stage_e(u):
        c, h, j, i, m = split(u)

        @pl.when(jnp.logical_not(handles(u)))
        def _():
            x_copy(u).wait_recv()
            s_copy(u).wait_recv()
            rows = pl.ds(mine, T)
            scale = s_recv[u, pl.ds(0, 1), :]
            scaled = (w32[i, rows] - step_in[h] * x_recv[u].astype(F32)) * scale

            @pl.when(c == 0)
            def _():
                w32[i, rows] = scaled
                w16[6 + i, rows] = scaled.astype(BF16)
                half_copy(u, i, theirs).wait_recv()

            @pl.when(c == 1)
            def _():
                w_out[h, j] = scaled

            d_copy(u).wait_send()

        @pl.when(handles(u))
        def _():
            x_copy(u).wait_send()
            s_copy(u).wait_send()

            @pl.when(c == 0)
            def _():
                half_copy(u, i, mine).wait_send()

        wait_rows(0, u, T, True)
        wait_rows(1, u, ROWS_1, True)
        wait_rows(2, u, ROWS_2, True)
        wait_rows(3, u, ROWS_2, True)
        wait_rows(4, u, ROWS_1, True)

    first = device == 0
    near = col_id <= row_id

    def fill(c, h):
        base = c * 6 + h * 3
        lanes = pl.ds(pl.multiple_of(h * DH, DH), DH)
        unit = unit_rows(qv[c, :, lanes])
        gate = dot(unit, w16[base])
        up = dot(unit, w16[base + 1])
        hidden = (gate * jax.nn.sigmoid(gate) * up).astype(BF16)
        recall[...] = dot(hidden, w16[base + 2])

        @pl.when(h == 0)
        def _():
            @pl.loop(0, 4)
            def _(n):
                for which in range(2):
                    halo_copy(c * 8 + 2 * n + which, which).wait_recv()

        hc = jnp.maximum(c - first.astype(jnp.int32), 0)
        bias = jnp.where(jnp.logical_and(first, c == 0), -1e30, 0.0)
        for a in range(4):
            part = pl.ds(pl.multiple_of(h * DH + a * HEAD_DIM, HEAD_DIM), HEAD_DIM)
            query = qv[c, :, part]
            here = dot(query, kv[c, :, part], ((1,), (1,)))
            there = dot(query, halo[0, hc, :, part], ((1,), (1,)))
            scale = HEAD_DIM ** (-0.5)
            scores = jnp.where(near, here * scale, there * scale + bias)
            top = jnp.max(scores, axis=-1, keepdims=True)
            expo = jnp.exp(scores - top)
            probs = expo / jnp.sum(expo, axis=-1, keepdims=True)
            near_probs = jnp.where(near, probs, 0.0).astype(BF16)
            far_probs = jnp.where(near, 0.0, probs).astype(BF16)
            result = dot(near_probs, vv[c, :, part]) + dot(far_probs, halo[1, hc, :, part])
            local = pl.ds(a * HEAD_DIM, HEAD_DIM)
            mixed_out[c, :, part] = (recall[:, local] + result).astype(BF16)

    def stage_h(n):
        for which in range(2):
            @pl.when(lax.rem(n, 2) == which)
            def _(which=which):
                halo_copy(n, which).start()

    def stage_m(_):
        @pl.loop(0, 6)
        def _(i):
            m_copy(i).wait()

        @pl.loop(0, 3)
        def _(t):
            m_send[t] = m32[matrix(2 * t + other), pl.ds(mine, T)].astype(BF16)
            m_remote(t).start()

    stages = {
        "A": stage_a, "B1": stage_b1, "B2": stage_b2, "C1": stage_c1, "C2": stage_c2,
        "D": stage_d, "NA": stage_na, "NB": stage_nb, "E": stage_e, "H": stage_h, "M": stage_m,
        "F": lambda f: fill(lax.div(f, 2), lax.rem(f, 2)),
    }

    def body(i, carry):
        words, units = carry
        later_words, later_units = [], []
        for (name, plan), word, unit in zip(PLAN, words, units):
            for n in range(1, len(plan)):
                word = jnp.where(i == 30 * n, plan[n], word)
            bit = lax.bitwise_and(word, 1)

            @pl.when(bit == 1)
            def _(name=name, unit=unit):
                stages[name](unit)

            later_words.append(lax.shift_right_logical(word, 1))
            later_units.append(unit + bit)
        return tuple(later_words), tuple(later_units)

    start_words = tuple(jnp.int32(plan[0]) for _, plan in PLAN)
    starts = tuple(jnp.int32(EARLY if name == "H" else 0) for name, _ in PLAN)
    lax.fori_loop(0, STEPS, body, (start_words, starts))

    @pl.loop(0, 6)
    def _(i):
        w_send(i).wait_send()

    @pl.loop(0, 3)
    def _(t):
        m_remote(t).wait_send()

    @pl.loop(0, 8)
    def _(n):
        for which in range(2):
            halo_copy(2 * n + which, which).wait_send()


def shards(queries, keys, values, token_lr, momentum_rate, update_step, fast_weights, momentum):
    hbm = pl.BlockSpec(memory_space=pl.ANY)
    vmem = pl.BlockSpec(memory_space=pltpu.VMEM)
    smem = pl.BlockSpec(memory_space=pltpu.SMEM)
    dma = pltpu.SemaphoreType.DMA
    return pl.pallas_call(
        kernel,
        out_shape=(
            pltpu.VMEM(queries.shape, BF16),
            pltpu.VMEM(fast_weights.shape, F32),
            pltpu.VMEM(momentum.shape, F32),
        ),
        in_specs=[hbm, hbm, hbm, vmem, smem, smem, hbm, hbm],
        out_specs=(vmem, vmem, vmem),
        scratch_shapes=[
            pltpu.VMEM((2, T, 1024), BF16),
            pltpu.VMEM((2, T, 1024), BF16),
            pltpu.VMEM((2, T, 1024), BF16),
            pltpu.VMEM((2, 2, T, 1024), BF16),
            pltpu.VMEM((T, DH), F32),
            pltpu.VMEM((6, DH, DH), F32),
            pltpu.VMEM((6, DH, DH), F32),
            pltpu.VMEM((12, DH, DH), BF16),
            pltpu.VMEM((3, T, DH), BF16),
            pltpu.VMEM((3, T, DH), BF16),
            pltpu.VMEM((2, T, DH), BF16),
            pltpu.VMEM((3, T, DH), BF16),
            pltpu.VMEM((6, T, DH), BF16),
            pltpu.VMEM((UNITS, T, DH), BF16),
            pltpu.VMEM((6, T, DH), F32),
            pltpu.VMEM((6, T, DH), BF16),
            pltpu.VMEM((UNITS, 192, DH), BF16),
            pltpu.VMEM((6, 128, DH), BF16),
            pltpu.VMEM((UNITS, 96, DH), BF16),
            pltpu.VMEM((UNITS, DH, DH), BF16),
            pltpu.VMEM((DH, DH), BF16),
            pltpu.VMEM((DH, DH), F32),
            pltpu.VMEM((DH, DH), BF16),
            pltpu.VMEM((DH, DH), BF16),
            pltpu.VMEM((6, T, DH), BF16),
            pltpu.VMEM((UNITS, T, DH), BF16),
            pltpu.VMEM((6, 8, DH), F32),
            pltpu.VMEM((UNITS, 8, DH), F32),
            dma((3,)), dma((6,)), dma((6,)), dma((6,)), dma((6,)), dma((3,)), dma((3,)),
            dma((16,)), dma((16,)),
            dma((9, UNITS)), dma((9, UNITS)),
        ],
        compiler_params=pltpu.CompilerParams(
            collective_id=0, has_side_effects=True, vmem_limit_bytes=58_700_000
        ),
    )(queries, keys, values, token_lr, momentum_rate, update_step, fast_weights, momentum)


def solution(mesh):
    wide = P(None, ("tok", "row"), "mem")
    state = P("mem", None, "row", None)
    return jax.shard_map(
        shards,
        mesh=mesh,
        in_specs=(wide, wide, wide, P("mem", None, ("tok", "row")), P("mem"), P("mem"), state, state),
        out_specs=(wide, state, state),
        check_vma=False,
    )
```

```python
import jax
import jax.numpy as jnp
from jax import lax
from jax.experimental import pallas as pl
from jax.experimental.pallas import tpu as pltpu
from jax.sharding import PartitionSpec as P

DH = 512
HEAD_DIM = 128
QUINTIC = (3.4445, -4.775, 2.0315)
MESH = pl.DeviceIdType.MESH
F32 = jnp.float32
BF16 = jnp.bfloat16
T = 256
UNITS = 12
ZC, XC = 256, 256
ROWS_1 = (128 * ZC + 192 * XC) // DH
ROWS_2 = (96 * ZC + 32 * XC) // DH

EARLY = 8
STEPS = 56
PLAN = (
    ("E", (58720256, 65077276,)),
    ("D", (611352576, 1746944,)),
    ("H", (93192192, 9,)),
    ("NA", (560988160, 3563521,)),
    ("A", (234881119, 112,)),
    ("C1", (2243584, 14896,)),
    ("F", (20480, 1280,)),
    ("B2", (75648, 1806,)),
    ("B1", (939526776, 224,)),
    ("C2", (21082112, 92800,)),
    ("NB", (611319808, 3842049,)),
    ("M", (128, 0,)),
)


def dot(a, b, dims=((1,), (0,))):
    return lax.dot_general(a, b, (dims, ((), ())), preferred_element_type=F32)


def unit_rows(field):
    field = field.astype(F32)
    return (field * lax.rsqrt(jnp.mean(field * field, axis=-1, keepdims=True) + 1e-05)).astype(BF16)


def kernel(
    q_in, k_in, v_in, lr_in, rate_in, step_in, w_in, m_in,
    mixed_out, w_out, m_out,
    qv, kv, vv, halo, recall, w32, m32, w16, m_send, m_recv,
    left, right, send_a, recv_a, own, send_b, recv_b1, send_b2, recv_b2, total,
    ortho, gram, gram16, poly, x_send, x_recv, s_send, s_recv,
    load_sem, w_load, m_load, w_ssem, w_rsem, m_ssem, m_rsem, h_ssem, h_rsem,
    ssem, rsem,
):
    tok = lax.axis_index("tok")
    row = lax.axis_index("row")
    x = lax.rem(tok, 4)
    z = lax.div(tok, 4)
    other = 1 - row
    z_tok = lax.rem(tok + 4, 8)
    device = tok * 2 + row
    after = lax.rem(device + 1, 16)
    before = lax.rem(device + 15, 16)
    mine = pl.multiple_of(row * T, T)
    theirs = pl.multiple_of(other * T, T)

    def chip(t):
        return {"tok": t, "row": row}

    partner = {"tok": tok, "row": other}
    z_peer = chip(z_tok)
    next_dev = {"tok": lax.div(after, 2), "row": lax.rem(after, 2)}
    prev_dev = {"tok": lax.div(before, 2), "row": lax.rem(before, 2)}

    def x_of(k):
        return lax.rem(x + k, 4)

    def x_peer(k):
        return chip(z * 4 + x_of(k))

    def remote(src, dst, send, recv, target):
        return pltpu.make_async_remote_copy(
            src_ref=src, dst_ref=dst, send_sem=send, recv_sem=recv,
            device_id=target, device_id_type=MESH,
        )

    barrier = pltpu.get_barrier_semaphore()
    for target in (partner, x_peer(1), x_peer(2), x_peer(3), z_peer, next_dev, prev_dev):
        pl.semaphore_signal(barrier, inc=1, device_id=target, device_id_type=MESH)

    def w_copy(i):
        return pltpu.make_async_copy(
            w_in.at[lax.div(i, 3), lax.rem(i, 3)], w32.at[i, pl.ds(mine, T)], w_load.at[i]
        )

    def m_copy(i):
        return pltpu.make_async_copy(
            m_in.at[lax.div(i, 3), lax.rem(i, 3)], m32.at[i, pl.ds(mine, T)], m_load.at[i]
        )

    k_copy = pltpu.make_async_copy(k_in, kv, load_sem.at[0])
    v_copy = pltpu.make_async_copy(v_in, vv, load_sem.at[1])
    q_copy = pltpu.make_async_copy(q_in, qv, load_sem.at[2])

    @pl.loop(0, 6)
    def _(i):
        w_copy(i).start()

    k_copy.start()
    v_copy.start()

    @pl.loop(0, 6)
    def _(i):
        m_copy(i).start()

    q_copy.start()

    pl.semaphore_wait(barrier, 7)

    def w_send(i):
        block = w16.at[i, pl.ds(mine, T)]
        return remote(block, block, w_ssem.at[i], w_rsem.at[i], partner)

    def m_remote(t):
        return remote(m_send.at[t], m_recv.at[t], m_ssem.at[t], m_rsem.at[t], partner)

    def matrix(m):
        return lax.div(m, 3) * 3 + lax.rem(lax.rem(m, 3) + 2, 3)

    def halo_copy(n, which):
        c = lax.div(n, 8)
        source = (k_in, v_in)[which]
        rows = pl.ds(pl.multiple_of(lax.rem(lax.div(n, 2), 4) * 64, 64), 64)
        return remote(
            source.at[c, rows], halo.at[which, c, rows], h_ssem.at[n], h_rsem.at[n], next_dev
        )

    for n in range(EARLY):
        halo_copy(jnp.int32(n), n % 2).start()

    @pl.loop(0, 6)
    def _(i):
        w_copy(i).wait()
        w16[i, pl.ds(mine, T)] = w32[i, pl.ds(mine, T)].astype(BF16)
        w_send(i).start()

    k_copy.wait()
    v_copy.wait()
    q_copy.wait()

    def split(u):
        c = lax.div(u, 6)
        m = lax.rem(u, 6)
        h = lax.div(m, 3)
        jj = lax.rem(m, 3)
        return c, h, lax.rem(jj + 2, 3), matrix(m), m

    row_id = lax.broadcasted_iota(jnp.int32, (T, T), 0)
    col_id = lax.broadcasted_iota(jnp.int32, (T, T), 1)

    def keys(u):
        c, h, _, _, _ = split(u)

        @pl.when(c == 0)
        def _():
            for j in range(3):
                w_send(h * 3 + j).wait_recv()

        base = c * 6 + h * 3
        lanes = pl.ds(pl.multiple_of(h * DH, DH), DH)
        unit = unit_rows(kv[c, :, lanes])
        left[1] = unit
        gate = dot(unit, w16[base])
        up = dot(unit, w16[base + 1])
        sig = jax.nn.sigmoid(gate)
        silu = gate * sig
        left[0] = (silu * up).astype(BF16)
        lr = lr_in[h, pl.ds(c, 1), :]
        lr = jnp.sum(jnp.where(row_id == col_id, lr, 0.0), axis=1, keepdims=True)
        target = (-(lr * vv[c, :, lanes].astype(F32))).astype(BF16)
        right[0] = target
        back = dot(target, w16[base + 2], ((1,), (1,)))
        right[1] = (back * up * sig * (1.0 + gate * (1.0 - sig))).astype(BF16)
        right[2] = (back * silu).astype(BF16)

    def a_copy(u):
        m = lax.rem(u, 6)
        return remote(send_a.at[m], recv_a.at[u], ssem.at[0, u], rsem.at[0, u], partner)

    def stage_a(u):
        @pl.when(lax.rem(u, 3) == 0)
        def _():
            keys(u)

        m = lax.rem(u, 6)
        jj = lax.rem(m, 3)
        li = jnp.minimum(jj, 1)
        rhs = right[jj]
        send_a[m] = dot(left[li, :, pl.ds(theirs, T)], rhs, ((0,), (0,))).astype(BF16)
        a_copy(u).start()
        own[m] = dot(left[li, :, pl.ds(mine, T)], rhs, ((0,), (0,)))

    def wait_rows(stage, u, rows, send):
        block = total.at[u, pl.ds(0, rows)]
        copy = remote(block, block, ssem.at[stage, u], rsem.at[stage, u], partner)
        if send:
            copy.wait_send()
        else:
            copy.wait_recv()

    z_cols, x_cols = pl.ds(0, ZC), pl.ds(ZC, XC)

    def stage_b1(u):
        m = lax.rem(u, 6)
        a_copy(u).wait_recv()
        summed = own[m] + recv_a[u].astype(F32)
        own[m] = summed
        send_b[m] = summed.astype(BF16)

        remote(
            send_b.at[m, pl.ds(pl.multiple_of((1 - z) * 128, 128), 128), z_cols],
            recv_b1.at[u, pl.ds(0, 128), z_cols], ssem.at[1, u], rsem.at[1, u], z_peer,
        ).start()
        for k in (2, 1, 3):
            remote(
                send_b.at[m, pl.ds(pl.multiple_of(x_of(k) * 64, 64), 64), x_cols],
                recv_b1.at[u, pl.ds((k - 1) * 64, 64), x_cols],
                ssem.at[1, u], rsem.at[1, u], x_peer(k),
            ).start()

    def stage_b2(u):
        m = lax.rem(u, 6)
        wait_rows(1, u, ROWS_1, False)
        keep = pl.ds(pl.multiple_of(z * 128, 128), 128)
        summed = own[m, keep, z_cols] + recv_b1[u, pl.ds(0, 128), z_cols].astype(F32)
        own[m, keep, z_cols] = summed
        send_b2[m, :, z_cols] = summed.astype(BF16)
        for k in (2, 1, 3):
            remote(
                send_b2.at[m, pl.ds(pl.multiple_of(x_of(k) * 32, 32), 32), z_cols],
                recv_b2.at[u, pl.ds((k - 1) * 32, 32), z_cols],
                ssem.at[2, u], rsem.at[2, u], x_peer(k),
            ).start()
        keep = pl.ds(pl.multiple_of(x * 64, 64), 64)
        summed = own[m, keep, x_cols]
        for k in range(3):
            summed = summed + recv_b1[u, pl.ds(k * 64, 64), x_cols].astype(F32)
        own[m, keep, x_cols] = summed
        send_b2[m, pl.ds(0, 64), x_cols] = summed.astype(BF16)
        remote(
            send_b2.at[m, pl.ds(pl.multiple_of((1 - z) * 32, 32), 32), x_cols],
            recv_b2.at[u, pl.ds(0, 32), x_cols], ssem.at[2, u], rsem.at[2, u], z_peer,
        ).start()

    def stage_c1(u):
        m = lax.rem(u, 6)
        wait_rows(2, u, ROWS_2, False)
        for place, cols, count in ((z * 128 + x * 32, z_cols, 3), (x * 64 + z * 32, x_cols, 1)):
            summed = own[m, pl.ds(pl.multiple_of(place, 32), 32), cols]
            for k in range(count):
                summed = summed + recv_b2[u, pl.ds(k * 32, 32), cols].astype(F32)
            at = pl.ds(pl.multiple_of(row * T + place, 32), 32)
            total[u, at, cols] = summed.astype(BF16)
            block = total.at[u, at, cols]
            for target in (x_peer(2), x_peer(1), x_peer(3)) if count == 3 else (z_peer,):
                remote(block, block, ssem.at[3, u], rsem.at[3, u], target).start()

    def stage_c2(u):
        wait_rows(3, u, ROWS_2, False)
        block = total.at[u, pl.ds(pl.multiple_of(row * T + z * 128, 128), 128), z_cols]
        remote(block, block, ssem.at[4, u], rsem.at[4, u], z_peer).start()
        block = total.at[u, pl.ds(pl.multiple_of(row * T + x * 64, 64), 64), x_cols]
        for k in (2, 1, 3):
            remote(block, block, ssem.at[4, u], rsem.at[4, u], x_peer(k)).start()

    def handles(u):
        return lax.rem(u, 2) == row

    def d_copy(u):
        block = total.at[u, pl.ds(mine, T)]
        return remote(block, block, ssem.at[5, u], rsem.at[5, u], partner)

    def stage_d(u):
        wait_rows(4, u, ROWS_1, False)

        @pl.when(jnp.logical_not(handles(u)))
        def _():
            d_copy(u).start()

    def newton_schulz():
        for b in range(4):
            rows = pl.ds(b * 128, 128)
            part = dot(ortho[:, rows], ortho[...], ((0,), (0,)))
            gram[rows] = part
            gram16[rows] = part.astype(BF16)
        for b in range(4):
            rows = pl.ds(b * 128, 128)
            square = dot(gram16[rows], gram16[...])
            poly[rows] = (QUINTIC[1] * gram[rows] + QUINTIC[2] * square).astype(BF16)
        for b in range(4):
            rows = pl.ds(b * 128, 128)
            old = ortho[rows]
            turned = dot(old, poly[...])
            ortho[rows] = (QUINTIC[0] * old.astype(F32) + turned).astype(BF16)

    def stage_na(u):
        c, h, j, i, m = split(u)
        rate = rate_in[h]

        @pl.when(handles(u))
        def _():
            wait_rows(5, u, T, False)

            @pl.when(c == 0)
            def _():
                t = lax.div(m, 2)
                m_remote(t).wait_recv()
                m32[i, pl.ds(theirs, T)] = m_recv[t].astype(F32)

            squares = jnp.zeros((1, DH), F32)
            for b in range(4):
                rows = pl.ds(b * 128, 128)
                moment = rate * m32[i, rows] + total[u, rows].astype(F32)
                m32[i, rows] = moment
                squares = squares + jnp.sum(moment * moment, axis=0, keepdims=True)
            inverse = lax.rsqrt(jnp.sum(squares, axis=1, keepdims=True) + 1e-06)
            for b in range(4):
                rows = pl.ds(b * 128, 128)
                ortho[rows] = (m32[i, rows] * inverse).astype(BF16)

            @pl.when(c == 1)
            def _():
                m_out[h, j] = m32[i, pl.ds(mine, T)]

            newton_schulz()

        @pl.when(jnp.logical_not(handles(u)))
        def _():
            rows = pl.ds(mine, T)
            moment = rate * m32[i, rows] + total[u, rows].astype(F32)
            m32[i, rows] = moment

            @pl.when(c == 1)
            def _():
                m_out[h, j] = moment

    def x_copy(u):
        return remote(
            x_send.at[lax.rem(u, 6)], x_recv.at[u], ssem.at[6, u], rsem.at[6, u], partner
        )

    def s_copy(u):
        return remote(
            s_send.at[lax.rem(u, 6)], s_recv.at[u], ssem.at[7, u], rsem.at[7, u], partner
        )

    def half_copy(u, i, start):
        block = w16.at[6 + i, pl.ds(start, T)]
        return remote(block, block, ssem.at[8, u], rsem.at[8, u], partner)

    def stage_nb(u):
        c, h, j, i, m = split(u)

        @pl.when(handles(u))
        def _():
            @pl.when(c == 0)
            def _():
                w32[i, pl.ds(theirs, T)] = w16[i, pl.ds(theirs, T)].astype(F32)

            newton_schulz()
            x_send[m] = ortho[pl.ds(theirs, T)]
            x_copy(u).start()
            step = step_in[h]
            columns = jnp.zeros((1, DH), F32)
            for b in range(4):
                rows = pl.ds(b * 128, 128)
                stepped = w32[i, rows] - step * ortho[rows].astype(F32)
                w32[i, rows] = stepped
                columns = columns + jnp.sum(stepped * stepped, axis=0, keepdims=True)
            scale = lax.rsqrt(columns + 1e-06)
            s_send[m] = jnp.broadcast_to(scale, (8, DH))
            s_copy(u).start()

            @pl.when(c == 0)
            def _():
                for start in (mine, theirs):
                    for b in range(2):
                        rows = pl.ds(pl.multiple_of(start + b * 128, 128), 128)
                        scaled = w32[i, rows] * scale
                        w32[i, rows] = scaled
                        w16[6 + i, rows] = scaled.astype(BF16)
                    if start is mine:
                        half_copy(u, i, mine).start()

            @pl.when(c == 1)
            def _():
                w_out[h, j] = w32[i, pl.ds(mine, T)] * scale

    def stage_e(u):
        c, h, j, i, m = split(u)

        @pl.when(jnp.logical_not(handles(u)))
        def _():
            x_copy(u).wait_recv()
            s_copy(u).wait_recv()
            rows = pl.ds(mine, T)
            scale = s_recv[u, pl.ds(0, 1), :]
            scaled = (w32[i, rows] - step_in[h] * x_recv[u].astype(F32)) * scale

            @pl.when(c == 0)
            def _():
                w32[i, rows] = scaled
                w16[6 + i, rows] = scaled.astype(BF16)
                half_copy(u, i, theirs).wait_recv()

            @pl.when(c == 1)
            def _():
                w_out[h, j] = scaled

            d_copy(u).wait_send()

        @pl.when(handles(u))
        def _():
            x_copy(u).wait_send()
            s_copy(u).wait_send()

            @pl.when(c == 0)
            def _():
                half_copy(u, i, mine).wait_send()

        wait_rows(0, u, T, True)
        wait_rows(1, u, ROWS_1, True)
        wait_rows(2, u, ROWS_2, True)
        wait_rows(3, u, ROWS_2, True)
        wait_rows(4, u, ROWS_1, True)

    first = device == 0
    near = col_id <= row_id

    def fill(c, h):
        base = c * 6 + h * 3
        lanes = pl.ds(pl.multiple_of(h * DH, DH), DH)
        unit = unit_rows(qv[c, :, lanes])
        gate = dot(unit, w16[base])
        up = dot(unit, w16[base + 1])
        hidden = (gate * jax.nn.sigmoid(gate) * up).astype(BF16)
        recall[...] = dot(hidden, w16[base + 2])

        @pl.when(h == 0)
        def _():
            @pl.loop(0, 4)
            def _(n):
                for which in range(2):
                    halo_copy(c * 8 + 2 * n + which, which).wait_recv()

        hc = jnp.maximum(c - first.astype(jnp.int32), 0)
        bias = jnp.where(jnp.logical_and(first, c == 0), -1e30, 0.0)
        for a in range(4):
            part = pl.ds(pl.multiple_of(h * DH + a * HEAD_DIM, HEAD_DIM), HEAD_DIM)
            query = qv[c, :, part]
            here = dot(query, kv[c, :, part], ((1,), (1,)))
            there = dot(query, halo[0, hc, :, part], ((1,), (1,)))
            scale = HEAD_DIM ** (-0.5)
            scores = jnp.where(near, here * scale, there * scale + bias)
            top = jnp.max(scores, axis=-1, keepdims=True)
            expo = jnp.exp(scores - top)
            probs = expo / jnp.sum(expo, axis=-1, keepdims=True)
            near_probs = jnp.where(near, probs, 0.0).astype(BF16)
            far_probs = jnp.where(near, 0.0, probs).astype(BF16)
            result = dot(near_probs, vv[c, :, part]) + dot(far_probs, halo[1, hc, :, part])
            local = pl.ds(a * HEAD_DIM, HEAD_DIM)
            mixed_out[c, :, part] = (recall[:, local] + result).astype(BF16)

    def stage_h(n):
        for which in range(2):
            @pl.when(lax.rem(n, 2) == which)
            def _(which=which):
                halo_copy(n, which).start()

    def stage_m(_):
        @pl.loop(0, 6)
        def _(i):
            m_copy(i).wait()

        @pl.loop(0, 3)
        def _(t):
            m_send[t] = m32[matrix(2 * t + other), pl.ds(mine, T)].astype(BF16)
            m_remote(t).start()

    stages = {
        "A": stage_a, "B1": stage_b1, "B2": stage_b2, "C1": stage_c1, "C2": stage_c2,
        "D": stage_d, "NA": stage_na, "NB": stage_nb, "E": stage_e, "H": stage_h, "M": stage_m,
        "F": lambda f: fill(lax.div(f, 2), lax.rem(f, 2)),
    }

    def body(i, carry):
        words, units = carry
        later_words, later_units = [], []
        for (name, plan), word, unit in zip(PLAN, words, units):
            for n in range(1, len(plan)):
                word = jnp.where(i == 30 * n, plan[n], word)
            bit = lax.bitwise_and(word, 1)

            @pl.when(bit == 1)
            def _(name=name, unit=unit):
                stages[name](unit)

            later_words.append(lax.shift_right_logical(word, 1))
            later_units.append(unit + bit)
        return tuple(later_words), tuple(later_units)

    start_words = tuple(jnp.int32(plan[0]) for _, plan in PLAN)
    starts = tuple(jnp.int32(EARLY if name == "H" else 0) for name, _ in PLAN)
    lax.fori_loop(0, STEPS, body, (start_words, starts))

    @pl.loop(0, 6)
    def _(i):
        w_send(i).wait_send()

    @pl.loop(0, 3)
    def _(t):
        m_remote(t).wait_send()

    @pl.loop(0, 8)
    def _(n):
        for which in range(2):
            halo_copy(2 * n + which, which).wait_send()


def shards(queries, keys, values, token_lr, momentum_rate, update_step, fast_weights, momentum):
    hbm = pl.BlockSpec(memory_space=pl.ANY)
    vmem = pl.BlockSpec(memory_space=pltpu.VMEM)
    smem = pl.BlockSpec(memory_space=pltpu.SMEM)
    dma = pltpu.SemaphoreType.DMA
    return pl.pallas_call(
        kernel,
        out_shape=(
            pltpu.VMEM(queries.shape, BF16),
            pltpu.VMEM(fast_weights.shape, F32),
            pltpu.VMEM(momentum.shape, F32),
        ),
        in_specs=[hbm, hbm, hbm, vmem, smem, smem, hbm, hbm],
        out_specs=(vmem, vmem, vmem),
        scratch_shapes=[
            pltpu.VMEM((2, T, 1024), BF16),
            pltpu.VMEM((2, T, 1024), BF16),
            pltpu.VMEM((2, T, 1024), BF16),
            pltpu.VMEM((2, 2, T, 1024), BF16),
            pltpu.VMEM((T, DH), F32),
            pltpu.VMEM((6, DH, DH), F32),
            pltpu.VMEM((6, DH, DH), F32),
            pltpu.VMEM((12, DH, DH), BF16),
            pltpu.VMEM((3, T, DH), BF16),
            pltpu.VMEM((3, T, DH), BF16),
            pltpu.VMEM((2, T, DH), BF16),
            pltpu.VMEM((3, T, DH), BF16),
            pltpu.VMEM((6, T, DH), BF16),
            pltpu.VMEM((UNITS, T, DH), BF16),
            pltpu.VMEM((6, T, DH), F32),
            pltpu.VMEM((6, T, DH), BF16),
            pltpu.VMEM((UNITS, 192, DH), BF16),
            pltpu.VMEM((6, 128, DH), BF16),
            pltpu.VMEM((UNITS, 96, DH), BF16),
            pltpu.VMEM((UNITS, DH, DH), BF16),
            pltpu.VMEM((DH, DH), BF16),
            pltpu.VMEM((DH, DH), F32),
            pltpu.VMEM((DH, DH), BF16),
            pltpu.VMEM((DH, DH), BF16),
            pltpu.VMEM((6, T, DH), BF16),
            pltpu.VMEM((UNITS, T, DH), BF16),
            pltpu.VMEM((6, 8, DH), F32),
            pltpu.VMEM((UNITS, 8, DH), F32),
            dma((3,)), dma((6,)), dma((6,)), dma((6,)), dma((6,)), dma((3,)), dma((3,)),
            dma((16,)), dma((16,)),
            dma((9, UNITS)), dma((9, UNITS)),
        ],
        compiler_params=pltpu.CompilerParams(
            collective_id=0, has_side_effects=True, vmem_limit_bytes=58_700_000
        ),
    )(queries, keys, values, token_lr, momentum_rate, update_step, fast_weights, momentum)


def solution(mesh):
    wide = P(None, ("tok", "row"), "mem")
    state = P("mem", None, "row", None)
    return jax.shard_map(
        shards,
        mesh=mesh,
        in_specs=(wide, wide, wide, P("mem", None, ("tok", "row")), P("mem"), P("mem"), state, state),
        out_specs=(wide, state, state),
        check_vma=False,
    )
```
